512 devices in a mesh: fsdp: 64 (over y_hi, x, z), tp: 8 (over y_lo, core).
Axes of the slice: x: 4, y: 8 (y_hi: 2, y_lo: 4; y = y_hi * 4 + y_lo), z: 8, core: 2. Of those that a mesh axis runs over, the one named last changes fastest.
Arguments:
- grad_kv: bfloat16 [64, 4096, 1024], P('fsdp', None, 'tp'), may hold values from -4 to 4
- grad_gains: bfloat16 [64, 8, 8192], P('fsdp', 'tp'), may hold values from -4 to 4
- kv_weight: float32 [4096, 1024], P('fsdp', 'tp'), may hold values from -0.125 to 0.125
- kv_first: float32 [4096, 1024], P('fsdp', 'tp'), may hold values from -2 to 2
- kv_second: float32 [4096, 1024], P('fsdp', 'tp'), may hold values from 0.004 to 0.4
- gain_weight: float32 [8192], P(('fsdp', 'tp')), may hold values from 0.5 to 1.5
- gain_first: float32 [8192], P(('fsdp', 'tp')), may hold values from -2 to 2
- gain_second: float32 [8192], P(('fsdp', 'tp')), may hold values from 0.05 to 5
- average: bfloat16 [64, 64, 1024], P(None, 'tp'), may hold values from -0.125 to 0.125
Outputs:
- kv_weight_out: float32 [4096, 1024], P('fsdp', 'tp')
- kv_first_out: float32 [4096, 1024], P('fsdp', 'tp')
- kv_second_out: float32 [4096, 1024], P('fsdp', 'tp')
- gain_weight_out: float32 [8192], P(('fsdp', 'tp'))
- gain_first_out: float32 [8192], P(('fsdp', 'tp'))
- gain_second_out: float32 [8192], P(('fsdp', 'tp'))
- kv_blocks: bfloat16 [4096, 1024], P(None, 'tp')
- gain_copy: bfloat16 [8192], replicated
- average_out: bfloat16 [64, 64, 1024], P(None, 'tp')
The draws below stay inside these ranges and needn't reach their ends.
All inputs are finite; a program needn't handle non-finite values.
Results may differ from the reference program's by a relative error of at most 0.003.
Values may be sent and summed in bfloat16 or wider, within the bound.
No kernel may reach another device: no remote copies, remote signals or barrier semaphores. Data moves between devices by JAX's collectives and lax.ppermute only.
A program may use at most 64 MiB of HBM per device.

```python
import math
import jax
import jax.numpy as jnp
from jax import lax

D = 4096
STEP = 100
KVW = 1024
PARAMS = 4202496
SHARDS = 64
TPS = 8


def rising_scales(key, count):
    place = jnp.arange(count, dtype=jnp.float32) / count
    spread = jax.random.uniform(key, (count,), jnp.float32)
    return 3.0 ** place * 10.0 ** spread


def draw_grad_kv(key, part):
    keyed = jax.random.fold_in(key, 11)
    k_noise, k_rows, k_cols = jax.random.split(keyed, 3)
    rows = rising_scales(k_rows, D)
    cols = rising_scales(k_cols, KVW)
    base = 3.0 / (41.0 * math.sqrt(SHARDS))
    noise = jnp.clip(jax.random.normal(k_noise, (SHARDS, D, KVW), jnp.float32), -6.0, 6.0)
    values = noise * base * rows[None, :, None] * cols[None, None, :]
    return jnp.clip(values, -4.0, 4.0).astype(jnp.bfloat16)


def draw_grad_gains(key, part):
    keyed = jax.random.fold_in(key, 23)
    k_noise, k_rows = jax.random.split(keyed, 2)
    rows = rising_scales(k_rows, 2 * D)
    base = 2.0 / (8.8 * math.sqrt(SHARDS * TPS))
    noise = jnp.clip(jax.random.normal(k_noise, (SHARDS, TPS, 2 * D), jnp.float32), -6.0, 6.0)
    values = noise * base * rows[None, None, :]
    return jnp.clip(values, -4.0, 4.0).astype(jnp.bfloat16)


def shard_levels(key, shape, pieces, least, top_value):
    level = 1.0
    for axis_at, shards_of in pieces:
        steps = jax.random.uniform(jax.random.fold_in(jax.random.fold_in(key, 6), axis_at), (shards_of,), jnp.float32, least / len(pieces), top_value / len(pieces))
        level = level * jnp.repeat(jnp.exp(steps), shape[axis_at] // shards_of).reshape((-1,) + (1,) * (len(shape) - 1 - axis_at))
    return level


def scatter_about(rng, dims, width, limit, shards=(), kind=jnp.bfloat16):
    gain = shard_levels(rng, dims, shards, -0.22, 0.18) if shards else 1.0
    array = jax.random.normal(rng, dims, jnp.float32) * width * gain
    return jnp.minimum(jnp.maximum(array, -limit), limit).astype(kind)


def setup_inputs(seed: int = 0) -> dict:
    splits = jax.random.split(jax.random.key(seed), 10)
    grad_kv = draw_grad_kv(jax.random.fold_in(splits[9], 71), 0)
    grad_gains = draw_grad_gains(jax.random.fold_in(splits[9], 71), 0)
    kv_weight = scatter_about(splits[2], (D, KVW), 0.02, 0.125, ((0, 64), (1, 8)), jnp.float32)
    kv_first = scatter_about(splits[3], (D, KVW), 0.3, 2.0, ((0, 64), (1, 8)), jnp.float32)
    kv_second = jnp.clip(jnp.exp(math.log(0.4) - 4.6051702 * jax.random.uniform(splits[4], (D, KVW), jnp.float32) ** shard_levels(splits[4], (D, KVW), ((0, 64), (1, 8)), -0.2, 0.2)), 0.004, 0.4)
    gain_weight = jnp.clip(1.0 + 0.1 * jax.random.normal(splits[5], (2 * D,), jnp.float32), 0.5, 1.5)
    gain_first = scatter_about(splits[6], (2 * D,), 0.3, 2.0, ((0, 512),), jnp.float32)
    gain_second = jnp.clip(jnp.exp(math.log(5.0) - 4.6051702 * jax.random.uniform(splits[7], (2 * D,), jnp.float32) ** shard_levels(splits[7], (2 * D,), ((0, 512),), -0.2, 0.2)), 0.05, 5.0)
    average = scatter_about(splits[8], (SHARDS, D // SHARDS, KVW), 0.02, 0.125, ((1, 8),))
    return {"grad_kv": grad_kv, "grad_gains": grad_gains, "kv_weight": kv_weight, "kv_first": kv_first, "kv_second": kv_second, "gain_weight": gain_weight, "gain_first": gain_first, "gain_second": gain_second, "average": average}


def adam_update(grad, first, second, weight, factor, decay):
    clipped = factor * grad
    first_new = 0.9 * first + 0.1 * clipped
    second_new = 0.95 * second + 0.05 * clipped * clipped
    first_fix = 1.0 - 0.9 ** STEP
    second_fix = 1.0 - 0.95 ** STEP
    step_dir = first_new / first_fix / (jnp.sqrt(second_new / second_fix) + 1e-08)
    weight_new = weight - 0.001 * (step_dir + decay * weight)
    return (weight_new, first_new, second_new)

def reference(grad_kv, grad_gains, kv_weight, kv_first, kv_second, gain_weight, gain_first, gain_second, average):
    g_kv = lax.optimization_barrier(jnp.sum(grad_kv, axis=0, dtype=jnp.float32))
    g_gain = lax.optimization_barrier(jnp.sum(grad_gains, axis=(0, 1), dtype=jnp.float32))
    total = jnp.sum(g_kv * g_kv) + jnp.sum(g_gain * g_gain)
    factor = jnp.minimum(jnp.float32(1.0), 1.0 / jnp.sqrt(total / PARAMS + 1e-06))
    kv_w, kv_m, kv_v = adam_update(g_kv, kv_first, kv_second, kv_weight, factor, 0.1)
    gain_w, gain_m, gain_v = adam_update(g_gain, gain_first, gain_second, gain_weight, factor, 0.0)
    kv_blocks = kv_w.astype(jnp.bfloat16)
    gain_copy = gain_w.astype(jnp.bfloat16)
    blended = 0.8 * average.astype(jnp.float32) + 0.2 * kv_blocks.reshape(SHARDS, D // SHARDS, KVW).astype(jnp.float32)
    average_out = blended.astype(jnp.bfloat16)
    return (kv_w, kv_m, kv_v, gain_w, gain_m, gain_v, kv_blocks, gain_copy, average_out)
```

```python
import jax
import jax.numpy as jnp
from jax import lax
from jax.sharding import Mesh, PartitionSpec as P

STEP = 100
PARAMS = 4202496
F = ("yh", "x", "z")
T = ("yl", "c")
NY, NX, NZ, NT = 2, 4, 8, 8


def adam_update(grad, first, second, weight, factor, decay):
    clipped = factor * grad
    first_new = 0.9 * first + 0.1 * clipped
    second_new = 0.95 * second + 0.05 * clipped * clipped
    first_fix = 1.0 - 0.9**STEP
    second_fix = 1.0 - 0.95**STEP
    step_dir = first_new / first_fix / (jnp.sqrt(second_new / second_fix) + 1e-08)
    weight_new = weight - 0.001 * (step_dir + decay * weight)
    return (weight_new, first_new, second_new)


def spread(block, axes, count):
    return lax.all_to_all(
        jnp.broadcast_to(block[None], (count,) + block.shape), axes, 0, 0, tiled=True
    )


def swap(block):
    return lax.ppermute(block, "yh", [(0, 1), (1, 0)])


def shards(
    grad_kv,
    grad_gains,
    kv_weight,
    kv_first,
    kv_second,
    gain_weight,
    gain_first,
    gain_second,
    average,
):
    f32, bf16 = jnp.float32, jnp.bfloat16
    yh = lax.axis_index("yh")
    tp = lax.axis_index(T)
    rows, cols = kv_weight.shape
    slim = gain_weight.shape[0]
    slice_rows = rows // NT

    state = jnp.stack([kv_weight, kv_first, kv_second])
    gains = jnp.stack([gain_weight, gain_first, gain_second])
    peer_state = swap(state)
    peer_gains = swap(gains)

    terms = grad_kv.reshape(NY, NX, NZ, rows, cols).transpose(1, 2, 0, 3, 4)
    terms = terms.reshape(NX * NZ, NY * rows, cols)
    gain_terms = grad_gains.reshape(NY, NX * NZ, cols).transpose(1, 0, 2)
    pad = jnp.zeros((NX * NZ, 8 - NY, cols), bf16)
    sent = jnp.concatenate([terms, gain_terms, pad], axis=1)
    got = lax.all_to_all(sent, ("x", "z"), 0, 0, tiled=True)
    part = jnp.sum(got.astype(f32), axis=0)
    full = part + swap(part)
    piece = full[: NY * rows].reshape(NY, rows, cols)
    gain_part = full[NY * rows : NY * rows + NY]

    square = jnp.sum(piece * piece)
    misc = jnp.concatenate(
        [gain_part, jnp.full((1, cols), square), jnp.zeros((5, cols), f32)], axis=0
    )
    misc = jnp.sum(spread(misc, T, NT), axis=0)
    gain_full = misc[:NY]
    local = misc[NY] + jnp.sum(gain_full * gain_full)
    total = jnp.sum(spread(local[None], ("x", "z"), NX * NZ)[:, 0, 0])
    factor = jnp.minimum(f32(1.0), 1.0 / jnp.sqrt(total / PARAMS + 1e-06))

    own_g = jnp.where(yh == 0, piece[0], piece[1])
    peer_g = jnp.where(yh == 0, piece[1], piece[0])
    kv_w, kv_m, kv_v = adam_update(own_g, kv_first, kv_second, kv_weight, factor, 0.1)
    peer_w, _, _ = adam_update(
        peer_g, peer_state[1], peer_state[2], peer_state[0], factor, 0.1
    )
    gain_own = lax.dynamic_slice(gain_full, (0, tp * slim), (NY, slim))
    own_gg = jnp.where(yh == 0, gain_own[0], gain_own[1])
    peer_gg = jnp.where(yh == 0, gain_own[1], gain_own[0])
    gain_w, gain_m, gain_v = adam_update(
        own_gg, gain_first, gain_second, gain_weight, factor, 0.0
    )
    peer_gw, _, _ = adam_update(
        peer_gg, peer_gains[1], peer_gains[2], peer_gains[0], factor, 0.0
    )

    def ordered(own, peer):
        own, peer = own.astype(bf16), peer.astype(bf16)
        return jnp.where(yh == 0, jnp.stack([own, peer]), jnp.stack([peer, own]))

    new_kv = ordered(kv_w, peer_w)
    new_gain = ordered(gain_w, peer_gw)

    lanes = lax.broadcasted_iota(jnp.int32, (NY, cols), 1) // slim
    gain_lanes = jnp.where(lanes == tp, jnp.tile(new_gain, (1, NT)), bf16(0))
    to_tp = jnp.concatenate(
        [
            new_kv.reshape(NY, NT, slice_rows, cols)
            .transpose(1, 0, 2, 3)
            .reshape(NT, NY * slice_rows, cols),
            jnp.broadcast_to(gain_lanes[None], (NT, NY, cols)),
            jnp.zeros((NT, 8 - NY, cols), bf16),
        ],
        axis=1,
    )
    from_tp = lax.all_to_all(to_tp, T, 0, 0, tiled=True)
    avg_rows = from_tp[:, : NY * slice_rows].reshape(NT, NY, slice_rows, cols)
    avg_rows = avg_rows.transpose(1, 0, 2, 3).reshape(NY * rows, cols)
    gain_rows = jnp.sum(from_tp[:, NY * slice_rows :].astype(f32), axis=0).astype(bf16)

    block = jnp.concatenate([new_kv.reshape(NY * rows, cols), avg_rows, gain_rows], axis=0)
    block = spread(block, "z", NZ)
    block = spread(block, "x", NX)

    kv_blocks = block[:, :, : NY * rows].reshape(NX, NZ, NY, rows, cols)
    kv_blocks = kv_blocks.transpose(2, 0, 1, 3, 4).reshape(-1, cols)
    moved = block[:, :, NY * rows : 2 * NY * rows]
    moved = moved.reshape(NX, NZ, NY, NT, slice_rows, cols)
    moved = moved.transpose(2, 0, 1, 4, 3, 5).reshape(average.shape)
    gain_copy = block[:, :, 2 * NY * rows : 2 * NY * rows + NY]
    gain_copy = gain_copy.transpose(2, 0, 1, 3).reshape(-1)
    blended = 0.8 * average.astype(f32) + 0.2 * moved.astype(f32)
    average_out = blended.astype(bf16)
    return (kv_w, kv_m, kv_v, gain_w, gain_m, gain_v, kv_blocks, gain_copy, average_out)


def solution(mesh):
    fine = Mesh(mesh.devices.reshape(NY, NX, NZ, 4, 2), F + T)
    in_specs = (
        P(F, None, T),
        P(F, T, None),
        P(F, T),
        P(F, T),
        P(F, T),
        P(F + T),
        P(F + T),
        P(F + T),
        P(None, T, None),
    )
    out_specs = (
        P(F, T),
        P(F, T),
        P(F, T),
        P(F + T),
        P(F + T),
        P(F + T),
        P(None, T),
        P(),
        P(None, T, None),
    )
    return jax.shard_map(shards, mesh=fine, in_specs=in_specs, out_specs=out_specs, check_vma=False)
```

```python
import jax
import jax.numpy as jnp
from jax import lax
from jax.experimental import pallas as pl
from jax.experimental.pallas import tpu as pltpu
from jax.sharding import Mesh, PartitionSpec as P

STEP = 100
PARAMS = 4202496
F = ("yh", "x", "z")
T = ("yl", "c")
NY, NX, NZ, NT = 2, 4, 8, 8
ROWS, COLS = 64, 128
SL = ROWS // NT
KV = NY * ROWS
PACK = KV + 8
BLOCK = 2 * KV + 8
f32, bf16 = jnp.float32, jnp.bfloat16


def adam_update(grad, first, second, weight, factor, decay):
    clipped = factor * grad
    first_new = 0.9 * first + 0.1 * clipped
    second_new = 0.95 * second + 0.05 * clipped * clipped
    first_fix = 1.0 - 0.9**STEP
    second_fix = 1.0 - 0.95**STEP
    step_dir = first_new / first_fix / (jnp.sqrt(second_new / second_fix) + 1e-08)
    weight_new = weight - 0.001 * (step_dir + decay * weight)
    return (weight_new, first_new, second_new)


def sum_kernel(got_ref, misc_ref, part_ref, msg_ref):
    for r in range(0, PACK, SL):
        acc = got_ref[0, r : r + SL, :].astype(f32)
        for s in range(1, NX * NZ):
            acc += got_ref[s, r : r + SL, :].astype(f32)
        if r < KV:
            part_ref[r : r + SL, :] = acc
            p, t = divmod(r // SL, NT)
            for y in range(NY):
                msg_ref[y * NT + t, p * SL : (p + 1) * SL, :] = acc
        else:
            acc += misc_ref[...]
            for d in range(NY * NT):
                msg_ref[d, NY * SL : NY * SL + 8, :] = acc


def norm_kernel(got_ref, rows_ref, gain_ref, msg_ref):
    square = jnp.zeros((SL, COLS), f32)
    for p in range(NY):
        for t in range(NT):
            cut = slice(p * SL, (p + 1) * SL)
            g = got_ref[t, cut, :] + got_ref[NT + t, cut, :]
            rows_ref[p, t] = g
            square += g * g
    tail = slice(NY * SL, NY * SL + 8)
    halves = []
    for p in range(NY):
        acc = got_ref[p * NT, tail, :]
        for t in range(1, NT):
            acc += got_ref[p * NT + t, tail, :]
        halves.append(acc)
    both = halves[0] + halves[1]
    at = lax.broadcasted_iota(jnp.int32, (8, COLS), 0)
    gain_ref[0] = jnp.where(at < NY, both, halves[0])
    gain_ref[1] = jnp.where(at < NY, both, halves[1])
    square += jnp.where(at < NY, both * both * (1.0 / NT), 0.0)
    line = jnp.sum(square, axis=0, keepdims=True)
    msg_ref[...] = jnp.broadcast_to(line, msg_ref.shape)


def update_kernel(
    yh_ref, sums_ref, part_ref, peer_ref, state_ref, rows_ref, rstate_ref, gain_ref,
    w_ref, m_ref, v_ref, gout_ref, out_ref,
):
    total = jnp.sum(sums_ref[...])
    factor = jnp.minimum(
        f32(1.0), 1.0 / jnp.sqrt(jnp.full((1, COLS), total) / PARAMS + 1e-06)
    )
    yh = yh_ref[0]
    for p in range(NY):
        cut = slice(p * ROWS, (p + 1) * ROWS)
        g = part_ref[cut, :] + peer_ref[cut, :]
        w, m, v = adam_update(
            g, state_ref[p, 1], state_ref[p, 2], state_ref[p, 0], factor, 0.1
        )
        out_ref[cut, :] = w.astype(bf16)

        @pl.when(yh == p)
        def _():
            w_ref[...] = w
            m_ref[...] = m
            v_ref[...] = v

        for t in range(NT):
            w, _, _ = adam_update(
                rows_ref[p, t], rstate_ref[p, t, 1], rstate_ref[p, t, 2],
                rstate_ref[p, t, 0], factor, 0.1,
            )
            at = KV + p * ROWS + t * SL
            out_ref[at : at + SL, :] = w.astype(bf16)
    new = []
    for p in range(NY):
        rows = gain_ref[p]
        res = adam_update(
            rows[p : p + 1], rows[3:4], rows[4:5], rows[2:3], factor, 0.0
        )
        for k in range(3):
            gout_ref[p, k : k + 1, :] = res[k]
        new.append(res[0])
    out_ref[2 * KV :, :] = jnp.concatenate(
        new + [jnp.zeros((8 - NY, COLS), f32)], axis=0
    ).astype(bf16)


def final_kernel(got_ref, avg_ref, kv_ref, avg_out_ref, gain_ref):
    for p in range(NY):
        for z in range(NZ):
            kv_ref[p, 0, z] = got_ref[0, z, p * ROWS : (p + 1) * ROWS, :]
            for t in range(NT):
                at = KV + p * ROWS + t * SL
                lanes = slice(t * COLS, (t + 1) * COLS)
                new = got_ref[0, z, at : at + SL, :].astype(f32)
                old = avg_ref[p, 0, z, :, lanes].astype(f32)
                avg_out_ref[p, 0, z, :, lanes] = (0.8 * old + 0.2 * new).astype(bf16)
            gain_ref[p, 0, z : z + 1, :] = got_ref[0, z, 2 * KV + p : 2 * KV + p + 1, :]


def spread(block, axes, count):
    return lax.all_to_all(
        jnp.broadcast_to(block[None], (count,) + block.shape), axes, 0, 0, tiled=True
    )


def call(kernel, outs, *args, smem=0, flops=0):
    specs = [pl.BlockSpec(memory_space=pltpu.SMEM)] * smem
    specs += [pl.BlockSpec(memory_space=pltpu.VMEM)] * (len(args) - smem)
    moved = sum(a.size * a.dtype.itemsize for a in args)
    return pl.pallas_call(
        kernel,
        out_shape=[jax.ShapeDtypeStruct(s, d) for s, d in outs],
        in_specs=specs,
        out_specs=[pl.BlockSpec(memory_space=pltpu.VMEM)] * len(outs),
        compiler_params=pltpu.CompilerParams(vmem_limit_bytes=8 << 20),
        cost_estimate=pl.CostEstimate(flops=flops, bytes_accessed=moved, transcendentals=0),
    )(*args)


def shards(
    grad_kv,
    grad_gains,
    kv_weight,
    kv_first,
    kv_second,
    gain_weight,
    gain_first,
    gain_second,
    average,
):
    yh = lax.axis_index("yh")
    tp = lax.axis_index(T)
    slim = gain_weight.shape[0]

    state = lax.all_gather(
        jnp.stack([kv_weight, kv_first, kv_second]), ("yh",) + T, axis=0, tiled=False
    ).reshape(NY, NT, 3, ROWS, COLS)
    own_state = lax.dynamic_slice(
        state, (0, tp, 0, 0, 0), (NY, 1, 3, ROWS, COLS)
    ).reshape(NY, 3, ROWS, COLS)
    row_state = lax.dynamic_slice(
        state, (0, 0, 0, tp * SL, 0), (NY, NT, 3, SL, COLS)
    )
    lanes = lax.broadcasted_iota(jnp.int32, (3, COLS), 1) // slim
    gains = jnp.tile(jnp.stack([gain_weight, gain_first, gain_second]), (1, NT))
    gains = jnp.where(lanes == tp, gains, 0.0)
    misc = jnp.concatenate([jnp.zeros((2, COLS), f32), gains, jnp.zeros((3, COLS), f32)])

    terms = grad_kv.reshape(NY, NX, NZ, ROWS, COLS).transpose(1, 2, 0, 3, 4)
    terms = terms.reshape(NX * NZ, KV, COLS)
    gain_terms = grad_gains.reshape(NY, NX * NZ, COLS).transpose(1, 0, 2)
    pad = jnp.zeros((NX * NZ, 8 - NY, COLS), bf16)
    sent = jnp.concatenate([terms, gain_terms, pad], axis=1)
    got = lax.all_to_all(sent, ("x", "z"), 0, 0, tiled=True)
    part, msg = call(
        sum_kernel, [((KV, COLS), f32), ((NY * NT, NY * SL + 8, COLS), f32)], got, misc
    )
    peer = lax.ppermute(part, "yh", [(0, 1), (1, 0)])

    got = lax.all_to_all(msg, ("yh",) + T, 0, 0, tiled=True)
    count = NX * NZ * NT
    rows, gain_rows, msg = call(
        norm_kernel,
        [((NY, NT, SL, COLS), f32), ((NY, 8, COLS), f32), ((count, COLS), f32)],
        got,
    )
    sums = lax.all_to_all(msg, ("x", "z") + T, 0, 0, tiled=True)

    kv_w, kv_m, kv_v, gain_new, block = call(
        update_kernel,
        [((ROWS, COLS), f32)] * 3 + [((NY, 8, COLS), f32), ((BLOCK, COLS), bf16)],
        yh.astype(jnp.int32).reshape(1),
        sums, part, peer, own_state, rows, row_state, gain_rows,
        smem=1,
    )
    own_gain = lax.dynamic_slice(gain_new, (yh, 0, tp * slim), (1, 3, slim))[0]

    block = spread(block, "z", NZ)
    block = spread(block, "x", NX)

    def at_x(*shape):
        return pl.BlockSpec((NY, 1) + shape, lambda i: (0, i) + (0,) * len(shape))

    kv_blocks, average_out, gain_copy = pl.pallas_call(
        final_kernel,
        grid=(NX,),
        in_specs=[
            pl.BlockSpec((1, NZ, BLOCK, COLS), lambda i: (i, 0, 0, 0)),
            at_x(NZ, SL, NT * COLS),
        ],
        out_specs=[at_x(NZ, ROWS, COLS), at_x(NZ, SL, NT * COLS), at_x(NZ, COLS)],
        out_shape=[
            jax.ShapeDtypeStruct((NY, NX, NZ, ROWS, COLS), bf16),
            jax.ShapeDtypeStruct((NY, NX, NZ, SL, NT * COLS), bf16),
            jax.ShapeDtypeStruct((NY, NX, NZ, COLS), bf16),
        ],
        compiler_params=pltpu.CompilerParams(vmem_limit_bytes=8 << 20),
    )(block, average.reshape(NY, NX, NZ, SL, NT * COLS))
    return (
        kv_w, kv_m, kv_v, own_gain[0], own_gain[1], own_gain[2],
        kv_blocks.reshape(-1, COLS), gain_copy.reshape(-1), average_out.reshape(average.shape),
    )


def solution(mesh):
    fine = Mesh(mesh.devices.reshape(NY, NX, NZ, 4, 2), F + T)
    in_specs = (
        P(F, None, T),
        P(F, T, None),
        P(F, T),
        P(F, T),
        P(F, T),
        P(F + T),
        P(F + T),
        P(F + T),
        P(None, T, None),
    )
    out_specs = (
        P(F, T),
        P(F, T),
        P(F, T),
        P(F + T),
        P(F + T),
        P(F + T),
        P(None, T),
        P(),
        P(None, T, None),
    )
    return jax.shard_map(shards, mesh=fine, in_specs=in_specs, out_specs=out_specs, check_vma=False)
```

```python
import jax
import jax.numpy as jnp
from jax import lax
from jax.experimental import pallas as pl
from jax.experimental.pallas import tpu as pltpu
from jax.sharding import Mesh, PartitionSpec as P

STEP = 100
PARAMS = 4202496
F = ("yh", "x", "z")
T = ("yl", "c")
NY, NX, NZ, NT = 2, 4, 8, 8
ROWS, COLS = 64, 128
SL = ROWS // NT
KV = NY * ROWS
PACK = KV + 8
ZR = NZ * ROWS
STATE = NY * SL + 8
BLOCK = 2 * KV + 8
f32, bf16 = jnp.float32, jnp.bfloat16


def adam_update(grad, first, second, weight, factor, decay):
    clipped = factor * grad
    first_new = 0.9 * first + 0.1 * clipped
    second_new = 0.95 * second + 0.05 * clipped * clipped
    first_fix = 1.0 - 0.9**STEP
    second_fix = 1.0 - 0.95**STEP
    step_dir = first_new / first_fix / (jnp.sqrt(second_new / second_fix) + 1e-08)
    weight_new = weight - 0.001 * (step_dir + decay * weight)
    return (weight_new, first_new, second_new)


def pack_kernel(grad_ref, gain_ref, out_ref, sems):
    copies = []
    for p in range(NY):
        for x in range(NX):
            copies.append(
                pltpu.make_async_copy(
                    grad_ref.at[pl.ds((p * NX + x) * ZR, ZR)],
                    out_ref.at[x, pl.ds(p * ZR, ZR)],
                    sems.at[p * NX + x],
                )
            )
            copies[-1].start()
    for p in range(NY):
        for x in range(NX):
            at = (p * NX + x) * NZ
            to = NY * ZR + p * NZ
            out_ref[x, to : to + NZ, :] = gain_ref[at : at + NZ, :]
    for copy in copies:
        copy.wait()


def x_kernel(got_ref, out_ref):
    def total(at, size):
        acc = got_ref[0, at : at + size, :].astype(f32)
        for s in range(1, NX):
            acc += got_ref[s, at : at + size, :].astype(f32)
        return acc

    tails = [total(NY * ZR + p * NZ, NZ) for p in range(NY)]
    for z in range(NZ):
        for p in range(NY):
            for r in range(0, ROWS, 16):
                out_ref[z, p * ROWS + r : p * ROWS + r + 16, :] = total(
                    p * ZR + z * ROWS + r, 16
                )
        rows = [tail[z : z + 1] for tail in tails]
        out_ref[z, KV:, :] = jnp.concatenate(
            rows + [jnp.zeros((8 - NY, COLS), f32)], axis=0
        )


def z_kernel(got_ref, misc_ref, w_ref, m_ref, v_ref, part_ref, msg_ref):
    for r in range(0, PACK, SL):
        acc = got_ref[0, r : r + SL, :]
        for s in range(1, NZ):
            acc += got_ref[s, r : r + SL, :]
        if r < KV:
            part_ref[r : r + SL, :] = acc
            p, t = divmod(r // SL, NT)
            for y in range(NY):
                msg_ref[y * NT + t, p * SL : (p + 1) * SL, :] = acc
        else:
            acc += misc_ref[...]
            for d in range(NY * NT):
                msg_ref[d, NY * SL : NY * SL + 8, :] = acc
    for t in range(NT):
        for k, ref in enumerate((w_ref, m_ref, v_ref)):
            rows = ref[t * SL : (t + 1) * SL, :]
            at = STATE + k * SL
            for y in range(NY):
                msg_ref[y * NT + t, at : at + SL, :] = rows


def norm_kernel(got_ref, rows_ref, gain_ref, msg_ref):
    square = jnp.zeros((SL, COLS), f32)
    for p in range(NY):
        for t in range(NT):
            cut = slice(p * SL, (p + 1) * SL)
            g = got_ref[t, cut, :] + got_ref[NT + t, cut, :]
            rows_ref[p, t] = g
            square += g * g
    tail = slice(NY * SL, NY * SL + 8)
    halves = []
    for p in range(NY):
        acc = got_ref[p * NT, tail, :]
        for t in range(1, NT):
            acc += got_ref[p * NT + t, tail, :]
        halves.append(acc)
    both = halves[0] + halves[1]
    at = lax.broadcasted_iota(jnp.int32, (8, COLS), 0)
    gain_ref[0] = jnp.where(at < NY, both, halves[0])
    gain_ref[1] = jnp.where(at < NY, both, halves[1])
    square += jnp.where(at < NY, both * both * (1.0 / NT), 0.0)
    line = jnp.sum(square, axis=0, keepdims=True)
    msg_ref[...] = jnp.broadcast_to(line, msg_ref.shape)


def update_kernel(
    yh_ref, sums_ref, part_ref, peer_ref, w0_ref, m0_ref, v0_ref, pstate_ref, rows_ref,
    got_ref, gain_ref, w_ref, m_ref, v_ref, gout_ref, out_ref,
):
    total = jnp.sum(sums_ref[...])
    factor = jnp.minimum(
        f32(1.0), 1.0 / jnp.sqrt(jnp.full((1, COLS), total) / PARAMS + 1e-06)
    )
    yh = yh_ref[0]
    own = pl.ds(pl.multiple_of(yh * ROWS, ROWS), ROWS)
    other = pl.ds(pl.multiple_of((1 - yh) * ROWS, ROWS), ROWS)
    w, m, v = adam_update(
        part_ref[own, :] + peer_ref[own, :], m0_ref[...], v0_ref[...], w0_ref[...], factor, 0.1
    )
    w_ref[...] = w
    m_ref[...] = m
    v_ref[...] = v
    out_ref[own, :] = w.astype(bf16)
    w, _, _ = adam_update(
        part_ref[other, :] + peer_ref[other, :],
        pstate_ref[1], pstate_ref[2], pstate_ref[0], factor, 0.1,
    )
    out_ref[other, :] = w.astype(bf16)
    for p in range(NY):
        for t in range(NT):
            old = [
                got_ref[p * NT + t, STATE + k * SL : STATE + (k + 1) * SL, :]
                for k in range(3)
            ]
            w, _, _ = adam_update(rows_ref[p, t], old[1], old[2], old[0], factor, 0.1)
            at = KV + p * ROWS + t * SL
            out_ref[at : at + SL, :] = w.astype(bf16)
    new = []
    for p in range(NY):
        rows = gain_ref[p]
        res = adam_update(
            rows[p : p + 1], rows[3:4], rows[4:5], rows[2:3], factor, 0.0
        )
        for k in range(3):
            gout_ref[p, k : k + 1, :] = res[k]
        new.append(res[0])
    out_ref[2 * KV :, :] = jnp.concatenate(
        new + [jnp.zeros((8 - NY, COLS), f32)], axis=0
    ).astype(bf16)


def final_kernel(got_ref, avg_ref, kv_ref, avg_out_ref, gain_ref):
    for p in range(NY):
        for z in range(NZ):
            kv_ref[p, 0, z] = got_ref[0, z, p * ROWS : (p + 1) * ROWS, :]
            for t in range(NT):
                at = KV + p * ROWS + t * SL
                lanes = slice(t * COLS, (t + 1) * COLS)
                new = got_ref[0, z, at : at + SL, :].astype(f32)
                old = avg_ref[p, 0, z, :, lanes].astype(f32)
                avg_out_ref[p, 0, z, :, lanes] = (0.8 * old + 0.2 * new).astype(bf16)
            gain_ref[p, 0, z : z + 1, :] = got_ref[0, z, 2 * KV + p : 2 * KV + p + 1, :]


def spread(block, axes, count):
    return lax.all_to_all(
        jnp.broadcast_to(block[None], (count,) + block.shape), axes, 0, 0, tiled=True
    )


def call(kernel, outs, *args, smem=0, hbm=0, scratch=()):
    specs = [pl.BlockSpec(memory_space=pltpu.SMEM)] * smem
    specs += [pl.BlockSpec(memory_space=pl.ANY)] * hbm
    specs += [pl.BlockSpec(memory_space=pltpu.VMEM)] * (len(args) - smem - hbm)
    moved = sum(a.size * a.dtype.itemsize for a in args)
    return pl.pallas_call(
        kernel,
        out_shape=[jax.ShapeDtypeStruct(s, d) for s, d in outs],
        in_specs=specs,
        out_specs=[pl.BlockSpec(memory_space=pltpu.VMEM)] * len(outs),
        scratch_shapes=scratch,
        compiler_params=pltpu.CompilerParams(vmem_limit_bytes=8 << 20),
        cost_estimate=pl.CostEstimate(flops=moved, bytes_accessed=moved, transcendentals=0),
    )(*args)


def shards(
    grad_kv,
    grad_gains,
    kv_weight,
    kv_first,
    kv_second,
    gain_weight,
    gain_first,
    gain_second,
    average,
):
    yh = lax.axis_index("yh")
    tp = lax.axis_index(T)
    slim = gain_weight.shape[0]

    lanes = lax.broadcasted_iota(jnp.int32, (3, COLS), 1) // slim
    gains = jnp.tile(jnp.stack([gain_weight, gain_first, gain_second]), (1, NT))
    gains = jnp.where(lanes == tp, gains, 0.0)
    misc = jnp.concatenate([jnp.zeros((2, COLS), f32), gains, jnp.zeros((3, COLS), f32)])

    swap = [(0, 1), (1, 0)]
    peer_state = lax.ppermute(jnp.stack([kv_weight, kv_first, kv_second]), "yh", swap)

    (sent,) = call(
        pack_kernel,
        [((NX, NY * ZR + NY * NZ, COLS), bf16)],
        grad_kv.reshape(-1, COLS),
        grad_gains.reshape(-1, COLS),
        hbm=1,
        scratch=[pltpu.SemaphoreType.DMA((NY * NX,))],
    )
    got = lax.all_to_all(sent, "x", 0, 0, tiled=True)
    (sent,) = call(x_kernel, [((NZ, PACK, COLS), f32)], got)
    got = lax.all_to_all(sent, "z", 0, 0, tiled=True)
    part, msg = call(
        z_kernel,
        [((KV, COLS), f32), ((NY * NT, STATE + 3 * SL, COLS), f32)],
        got, misc, kv_weight, kv_first, kv_second,
    )
    peer = lax.ppermute(part, "yh", swap)

    got = lax.all_to_all(msg, ("yh",) + T, 0, 0, tiled=True)
    count = NX * NZ * NT
    rows, gain_rows, msg = call(
        norm_kernel,
        [((NY, NT, SL, COLS), f32), ((NY, 8, COLS), f32), ((count, COLS), f32)],
        got,
    )
    sums = lax.all_to_all(msg, ("x", "z") + T, 0, 0, tiled=True)

    kv_w, kv_m, kv_v, gain_new, block = call(
        update_kernel,
        [((ROWS, COLS), f32)] * 3 + [((NY, 8, COLS), f32), ((BLOCK, COLS), bf16)],
        yh.astype(jnp.int32).reshape(1),
        sums, part, peer, kv_weight, kv_first, kv_second, peer_state, rows, got, gain_rows,
        smem=1,
    )
    own_gain = lax.dynamic_slice(gain_new, (yh, 0, tp * slim), (1, 3, slim))[0]

    block = spread(block, "z", NZ)
    block, own_gain = lax.optimization_barrier((block, own_gain))
    block = spread(block, "x", NX)

    def at_x(*shape):
        return pl.BlockSpec((NY, 1) + shape, lambda i: (0, i) + (0,) * len(shape))

    kv_blocks, average_out, gain_copy = pl.pallas_call(
        final_kernel,
        grid=(NX,),
        in_specs=[
            pl.BlockSpec((1, NZ, BLOCK, COLS), lambda i: (i, 0, 0, 0)),
            at_x(NZ, SL, NT * COLS),
        ],
        out_specs=[at_x(NZ, ROWS, COLS), at_x(NZ, SL, NT * COLS), at_x(NZ, COLS)],
        out_shape=[
            jax.ShapeDtypeStruct((NY, NX, NZ, ROWS, COLS), bf16),
            jax.ShapeDtypeStruct((NY, NX, NZ, SL, NT * COLS), bf16),
            jax.ShapeDtypeStruct((NY, NX, NZ, COLS), bf16),
        ],
        compiler_params=pltpu.CompilerParams(vmem_limit_bytes=8 << 20),
    )(block, average.reshape(NY, NX, NZ, SL, NT * COLS))
    return (
        kv_w, kv_m, kv_v, own_gain[0], own_gain[1], own_gain[2],
        kv_blocks.reshape(-1, COLS), gain_copy.reshape(-1), average_out.reshape(average.shape),
    )


def solution(mesh):
    fine = Mesh(mesh.devices.reshape(NY, NX, NZ, 4, 2), F + T)
    in_specs = (
        P(F, None, T),
        P(F, T, None),
        P(F, T),
        P(F, T),
        P(F, T),
        P(F + T),
        P(F + T),
        P(F + T),
        P(None, T, None),
    )
    out_specs = (
        P(F, T),
        P(F, T),
        P(F, T),
        P(F + T),
        P(F + T),
        P(F + T),
        P(None, T),
        P(),
        P(None, T, None),
    )
    return jax.shard_map(shards, mesh=fine, in_specs=in_specs, out_specs=out_specs, check_vma=False)
```

```python
import jax
import jax.numpy as jnp
from jax import lax
from jax.experimental import pallas as pl
from jax.experimental.pallas import tpu as pltpu
from jax.sharding import Mesh, PartitionSpec as P

STEP = 100
PARAMS = 4202496
F = ("yh", "x", "z")
T = ("yl", "c")
NY, NX, NZ, NT = 2, 4, 8, 8
ROWS, COLS = 64, 128
SL = ROWS // NT
KV = NY * ROWS
PACK = KV + 8
ZR = NZ * ROWS
STATE = NY * SL + 8
BLOCK = 2 * KV + 8
f32, bf16 = jnp.float32, jnp.bfloat16


def adam_update(grad, first, second, weight, factor, decay):
    clipped = factor * grad
    first_new = 0.9 * first + 0.1 * clipped
    second_new = 0.95 * second + 0.05 * clipped * clipped
    first_fix = 1.0 - 0.9**STEP
    second_fix = 1.0 - 0.95**STEP
    step_dir = first_new / first_fix / (jnp.sqrt(second_new / second_fix) + 1e-08)
    weight_new = weight - 0.001 * (step_dir + decay * weight)
    return (weight_new, first_new, second_new)


def pack_kernel(grad_ref, gain_ref, out_ref, sems):
    copies = []
    for p in range(NY):
        for x in range(NX):
            copies.append(
                pltpu.make_async_copy(
                    grad_ref.at[pl.ds((p * NX + x) * ZR, ZR)],
                    out_ref.at[x, pl.ds(p * ZR, ZR)],
                    sems.at[p * NX + x],
                )
            )
            copies[-1].start()
    for p in range(NY):
        for x in range(NX):
            at = (p * NX + x) * NZ
            to = NY * ZR + p * NZ
            out_ref[x, to : to + NZ, :] = gain_ref[at : at + NZ, :]
    for copy in copies:
        copy.wait()


def x_kernel(got_ref, out_ref):
    def total(at, size):
        acc = got_ref[0, at : at + size, :].astype(f32)
        for s in range(1, NX):
            acc += got_ref[s, at : at + size, :].astype(f32)
        return acc

    tails = [total(NY * ZR + p * NZ, NZ) for p in range(NY)]
    for z in range(NZ):
        for p in range(NY):
            for r in range(0, ROWS, 16):
                out_ref[z, p * ROWS + r : p * ROWS + r + 16, :] = total(
                    p * ZR + z * ROWS + r, 16
                )
        rows = [tail[z : z + 1] for tail in tails]
        out_ref[z, KV:, :] = jnp.concatenate(
            rows + [jnp.zeros((8 - NY, COLS), f32)], axis=0
        )


def z_kernel(got_ref, misc_ref, w_ref, m_ref, v_ref, pair_ref, msg_ref):
    for r in range(0, PACK, SL):
        acc = got_ref[0, r : r + SL, :]
        for s in range(1, NZ):
            acc += got_ref[s, r : r + SL, :]
        if r < KV:
            pair_ref[r : r + SL, :] = acc
            p, t = divmod(r // SL, NT)
            for y in range(NY):
                msg_ref[y * NT + t, p * SL : (p + 1) * SL, :] = acc
        else:
            acc += misc_ref[...]
            for d in range(NY * NT):
                msg_ref[d, NY * SL : NY * SL + 8, :] = acc
    for k, ref in enumerate((w_ref, m_ref, v_ref)):
        pair_ref[KV + k * ROWS : KV + (k + 1) * ROWS, :] = ref[...]
        for t in range(NT):
            rows = ref[t * SL : (t + 1) * SL, :]
            at = STATE + k * SL
            for y in range(NY):
                msg_ref[y * NT + t, at : at + SL, :] = rows


def norm_kernel(got_ref, rows_ref, gain_ref, msg_ref):
    square = jnp.zeros((SL, COLS), f32)
    for p in range(NY):
        for t in range(NT):
            cut = slice(p * SL, (p + 1) * SL)
            g = got_ref[t, cut, :] + got_ref[NT + t, cut, :]
            rows_ref[p, t] = g
            square += g * g
    tail = slice(NY * SL, NY * SL + 8)
    halves = []
    for p in range(NY):
        acc = got_ref[p * NT, tail, :]
        for t in range(1, NT):
            acc += got_ref[p * NT + t, tail, :]
        halves.append(acc)
    both = halves[0] + halves[1]
    at = lax.broadcasted_iota(jnp.int32, (8, COLS), 0)
    gain_ref[0] = jnp.where(at < NY, both, halves[0])
    gain_ref[1] = jnp.where(at < NY, both, halves[1])
    square += jnp.where(at < NY, both * both * (1.0 / NT), 0.0)
    line = jnp.sum(square, axis=0, keepdims=True)
    msg_ref[...] = jnp.broadcast_to(line, msg_ref.shape)


def update_kernel(
    at_ref, sums_ref, pair_ref, peer_ref, rows_ref, got_ref, gain_ref,
    w_ref, m_ref, v_ref, gw_ref, gm_ref, gv_ref, out_ref,
):
    total = jnp.sum(sums_ref[...])
    factor = jnp.minimum(
        f32(1.0), 1.0 / jnp.sqrt(jnp.full((1, COLS), total) / PARAMS + 1e-06)
    )
    yh, tp = at_ref[0], at_ref[1]

    def update(at, state_ref):
        old = [state_ref[KV + k * ROWS : KV + (k + 1) * ROWS, :] for k in range(3)]
        cut = pl.ds(pl.multiple_of(at * ROWS, ROWS), ROWS)
        new = adam_update(
            pair_ref[cut, :] + peer_ref[cut, :], old[1], old[2], old[0], factor, 0.1
        )
        out_ref[cut, :] = new[0].astype(bf16)
        return new

    w, m, v = update(yh, pair_ref)
    w_ref[...] = w
    m_ref[...] = m
    v_ref[...] = v
    update(1 - yh, peer_ref)
    for p in range(NY):
        for t in range(NT):
            old = [
                got_ref[p * NT + t, STATE + k * SL : STATE + (k + 1) * SL, :]
                for k in range(3)
            ]
            w, _, _ = adam_update(rows_ref[p, t], old[1], old[2], old[0], factor, 0.1)
            at = KV + p * ROWS + t * SL
            out_ref[at : at + SL, :] = w.astype(bf16)
    new = []
    for p in range(NY):
        rows = gain_ref[p]
        new.append(
            adam_update(rows[p : p + 1], rows[3:4], rows[4:5], rows[2:3], factor, 0.0)
        )
    slim = COLS // NT
    own = [jnp.where(yh == 0, a, b) for a, b in zip(*new)]
    own = jnp.concatenate(own + [jnp.zeros((5, COLS), f32)], axis=0)
    own = pltpu.roll(own, (COLS - tp * slim) % COLS, 1)
    for k, ref in enumerate((gw_ref, gm_ref, gv_ref)):
        ref[...] = own[k : k + 1, :slim]
    out_ref[2 * KV :, :] = jnp.concatenate(
        [new[0][0], new[1][0], jnp.zeros((8 - NY, COLS), f32)], axis=0
    ).astype(bf16)


def final_kernel(got_ref, avg_ref, kv_ref, avg_out_ref, gain_ref):
    for p in range(NY):
        for z in range(NZ):
            kv_ref[p, 0, z] = got_ref[0, z, p * ROWS : (p + 1) * ROWS, :]
            for t in range(NT):
                at = KV + p * ROWS + t * SL
                lanes = slice(t * COLS, (t + 1) * COLS)
                new = got_ref[0, z, at : at + SL, :].astype(f32)
                old = avg_ref[p, 0, z, :, lanes].astype(f32)
                avg_out_ref[p, 0, z, :, lanes] = (0.8 * old + 0.2 * new).astype(bf16)
            gain_ref[p, 0, z : z + 1, :] = got_ref[0, z, 2 * KV + p : 2 * KV + p + 1, :]


def spread(block, axes, count):
    return lax.all_to_all(
        jnp.broadcast_to(block[None], (count,) + block.shape), axes, 0, 0, tiled=True
    )


def call(kernel, outs, *args, smem=0, hbm=0, scratch=()):
    specs = [pl.BlockSpec(memory_space=pltpu.SMEM)] * smem
    specs += [pl.BlockSpec(memory_space=pltpu.HBM)] * hbm
    specs += [pl.BlockSpec(memory_space=pltpu.VMEM)] * (len(args) - smem - hbm)
    moved = sum(a.size * a.dtype.itemsize for a in args)
    return pl.pallas_call(
        kernel,
        out_shape=[jax.ShapeDtypeStruct(s, d) for s, d in outs],
        in_specs=specs,
        out_specs=[pl.BlockSpec(memory_space=pltpu.VMEM)] * len(outs),
        scratch_shapes=scratch,
        compiler_params=pltpu.CompilerParams(vmem_limit_bytes=8 << 20),
        cost_estimate=pl.CostEstimate(flops=moved, bytes_accessed=moved, transcendentals=0),
    )(*args)


def shards(
    grad_kv,
    grad_gains,
    kv_weight,
    kv_first,
    kv_second,
    gain_weight,
    gain_first,
    gain_second,
    average,
):
    yh = lax.axis_index("yh")
    tp = lax.axis_index(T)
    slim = gain_weight.shape[0]

    lanes = lax.broadcasted_iota(jnp.int32, (3, COLS), 1) // slim
    gains = jnp.tile(jnp.stack([gain_weight, gain_first, gain_second]), (1, NT))
    gains = jnp.where(lanes == tp, gains, 0.0)
    misc = jnp.concatenate([jnp.zeros((2, COLS), f32), gains, jnp.zeros((3, COLS), f32)])

    (sent,) = call(
        pack_kernel,
        [((NX, NY * ZR + NY * NZ, COLS), bf16)],
        grad_kv.reshape(-1, COLS),
        grad_gains.reshape(-1, COLS),
        hbm=1,
        scratch=[pltpu.SemaphoreType.DMA((NY * NX,))],
    )
    sent, misc = lax.optimization_barrier((sent, misc))
    got = lax.all_to_all(sent, "x", 0, 0, tiled=True)
    (sent,) = call(x_kernel, [((NZ, PACK, COLS), f32)], got)
    got = lax.all_to_all(sent, "z", 0, 0, tiled=True)
    pair, msg = call(
        z_kernel,
        [((KV + 3 * ROWS, COLS), f32), ((NY * NT, STATE + 3 * SL, COLS), f32)],
        got, misc, kv_weight, kv_first, kv_second,
    )
    peer = lax.ppermute(pair, "yh", [(0, 1), (1, 0)])

    got = lax.all_to_all(msg, ("yh",) + T, 0, 0, tiled=True)
    count = NX * NZ * NT
    rows, gain_rows, msg = call(
        norm_kernel,
        [((NY, NT, SL, COLS), f32), ((NY, 8, COLS), f32), ((count, COLS), f32)],
        got,
    )
    sums = lax.all_to_all(msg, ("x", "z") + T, 0, 0, tiled=True)

    kv_w, kv_m, kv_v, gain_w, gain_m, gain_v, block = call(
        update_kernel,
        [((ROWS, COLS), f32)] * 3 + [((1, slim), f32)] * 3 + [((BLOCK, COLS), bf16)],
        jnp.stack([yh, tp]).astype(jnp.int32),
        sums, pair, peer, rows, got, gain_rows,
        smem=1,
    )

    block = spread(block, "z", NZ)
    block = spread(block, "x", NX)

    def at_x(*shape):
        return pl.BlockSpec((NY, 1) + shape, lambda i: (0, i) + (0,) * len(shape))

    kv_blocks, average_out, gain_copy = pl.pallas_call(
        final_kernel,
        grid=(NX,),
        in_specs=[
            pl.BlockSpec((1, NZ, BLOCK, COLS), lambda i: (i, 0, 0, 0)),
            at_x(NZ, SL, NT * COLS),
        ],
        out_specs=[at_x(NZ, ROWS, COLS), at_x(NZ, SL, NT * COLS), at_x(NZ, COLS)],
        out_shape=[
            jax.ShapeDtypeStruct((NY, NX, NZ, ROWS, COLS), bf16),
            jax.ShapeDtypeStruct((NY, NX, NZ, SL, NT * COLS), bf16),
            jax.ShapeDtypeStruct((NY, NX, NZ, COLS), bf16),
        ],
        compiler_params=pltpu.CompilerParams(vmem_limit_bytes=8 << 20),
    )(block, average.reshape(NY, NX, NZ, SL, NT * COLS))
    return (
        kv_w, kv_m, kv_v, gain_w.reshape(-1), gain_m.reshape(-1), gain_v.reshape(-1),
        kv_blocks.reshape(-1, COLS), gain_copy.reshape(-1), average_out.reshape(average.shape),
    )


def solution(mesh):
    fine = Mesh(mesh.devices.reshape(NY, NX, NZ, 4, 2), F + T)
    in_specs = (
        P(F, None, T),
        P(F, T, None),
        P(F, T),
        P(F, T),
        P(F, T),
        P(F + T),
        P(F + T),
        P(F + T),
        P(None, T, None),
    )
    out_specs = (
        P(F, T),
        P(F, T),
        P(F, T),
        P(F + T),
        P(F + T),
        P(F + T),
        P(None, T),
        P(),
        P(None, T, None),
    )
    return jax.shard_map(shards, mesh=fine, in_specs=in_specs, out_specs=out_specs, check_vma=False)
```

```python
import jax
import jax.numpy as jnp
from jax import lax
from jax.experimental import pallas as pl
from jax.experimental.pallas import tpu as pltpu
from jax.sharding import Mesh, PartitionSpec as P

STEP = 100
PARAMS = 4202496
F = ("yh", "x", "z")
T = ("yl", "c")
NY, NX, NZ, NT = 2, 4, 8, 8
ROWS, COLS = 64, 128
SL = ROWS // NT
KV = NY * ROWS
PACK = KV + 8
STATE = NY * SL + 8
AVG = NY * (NT - 1) * SL
BLOCK = KV + AVG + 8
f32, bf16 = jnp.float32, jnp.bfloat16


def adam_update(grad, first, second, weight, factor, decay):
    clipped = factor * grad
    first_new = 0.9 * first + 0.1 * clipped
    second_new = 0.95 * second + 0.05 * clipped * clipped
    first_fix = 1.0 - 0.9**STEP
    second_fix = 1.0 - 0.95**STEP
    step_dir = first_new / first_fix / (jnp.sqrt(second_new / second_fix) + 1e-08)
    weight_new = weight - 0.001 * (step_dir + decay * weight)
    return (weight_new, first_new, second_new)


def pack_kernel(grad_ref, gain_ref, out_ref, tail_ref, sems):
    copies = [
        pltpu.make_async_copy(
            grad_ref.at[p, pl.ds(x * NZ, NZ)],
            out_ref.at[pl.ds(x * NZ, NZ), pl.ds(p * ROWS, ROWS)],
            sems.at[p * NX + x],
        )
        for p in range(NY)
        for x in range(NX)
    ]
    for copy in copies:
        copy.start()
    count = NX * NZ
    gains = gain_ref[...].astype(f32)
    zero = jnp.zeros((8 - NY, COLS), f32)
    for d in range(count):
        rows = [gains[p * count + d : p * count + d + 1] for p in range(NY)]
        tail_ref[d] = jnp.concatenate(rows + [zero], axis=0).astype(bf16)
    last = pltpu.make_async_copy(tail_ref, out_ref.at[:, pl.ds(KV, 8)], sems.at[NY * NX])
    last.start()
    for copy in copies:
        copy.wait()
    last.wait()


def sum_kernel(got_ref, misc_ref, w_ref, m_ref, v_ref, part_ref, msg_ref):
    for r in range(0, PACK, SL):
        acc = got_ref[0, r : r + SL, :].astype(f32)
        for s in range(1, NX * NZ):
            acc += got_ref[s, r : r + SL, :].astype(f32)
        if r < KV:
            part_ref[r : r + SL, :] = acc
            p, t = divmod(r // SL, NT)
            for y in range(NY):
                msg_ref[y * NT + t, p * SL : (p + 1) * SL, :] = acc
        else:
            acc += misc_ref[...]
            for d in range(NY * NT):
                msg_ref[d, NY * SL : NY * SL + 8, :] = acc
    for k, ref in enumerate((w_ref, m_ref, v_ref)):
        for t in range(NT):
            rows = ref[t * SL : (t + 1) * SL, :]
            at = STATE + k * SL
            for y in range(NY):
                msg_ref[y * NT + t, at : at + SL, :] = rows


def norm_kernel(got_ref, rows_ref, gain_ref, msg_ref):
    square = jnp.zeros((SL, COLS), f32)
    for p in range(NY):
        for t in range(NT):
            cut = slice(p * SL, (p + 1) * SL)
            g = got_ref[t, cut, :] + got_ref[NT + t, cut, :]
            rows_ref[p, t] = g
            square += g * g
    tail = slice(NY * SL, NY * SL + 8)
    halves = []
    for p in range(NY):
        acc = got_ref[p * NT, tail, :]
        for t in range(1, NT):
            acc += got_ref[p * NT + t, tail, :]
        halves.append(acc)
    both = halves[0] + halves[1]
    at = lax.broadcasted_iota(jnp.int32, (8, COLS), 0)
    gain_ref[0] = jnp.where(at < NY, both, halves[0])
    gain_ref[1] = jnp.where(at < NY, both, halves[1])
    square += jnp.where(at < NY, both * both * (1.0 / NT), 0.0)
    line = jnp.sum(square, axis=0, keepdims=True)
    msg_ref[...] = jnp.broadcast_to(line, msg_ref.shape)


def update_kernel(
    at_ref, sums_ref, part_ref, peer_ref, w0_ref, m0_ref, v0_ref, pstate_ref, rows_ref,
    got_ref, gain_ref, w_ref, m_ref, v_ref, gw_ref, gm_ref, gv_ref, out_ref,
):
    total = jnp.sum(sums_ref[...])
    factor = jnp.minimum(
        f32(1.0), 1.0 / jnp.sqrt(jnp.full((1, COLS), total) / PARAMS + 1e-06)
    )
    yh, tp = at_ref[0], at_ref[1]
    own = pl.ds(pl.multiple_of(yh * ROWS, ROWS), ROWS)
    other = pl.ds(pl.multiple_of((1 - yh) * ROWS, ROWS), ROWS)
    w, m, v = adam_update(
        part_ref[own, :] + peer_ref[own, :], m0_ref[...], v0_ref[...], w0_ref[...], factor, 0.1
    )
    w_ref[...] = w
    m_ref[...] = m
    v_ref[...] = v
    out_ref[own, :] = w.astype(bf16)
    w, _, _ = adam_update(
        part_ref[other, :] + peer_ref[other, :],
        pstate_ref[1], pstate_ref[2], pstate_ref[0], factor, 0.1,
    )
    out_ref[other, :] = w.astype(bf16)
    for p in range(NY):
        for k in range(1, NT):
            t = (tp + k) % NT
            old = [
                got_ref[p * NT + t, STATE + j * SL : STATE + (j + 1) * SL, :]
                for j in range(3)
            ]
            w, _, _ = adam_update(rows_ref[p, t], old[1], old[2], old[0], factor, 0.1)
            at = KV + (p * (NT - 1) + k - 1) * SL
            out_ref[at : at + SL, :] = w.astype(bf16)
    new = []
    for p in range(NY):
        rows = gain_ref[p]
        new.append(
            adam_update(rows[p : p + 1], rows[3:4], rows[4:5], rows[2:3], factor, 0.0)
        )
    slim = COLS // NT
    own = [jnp.where(yh == 0, a, b) for a, b in zip(*new)]
    own = jnp.concatenate(own + [jnp.zeros((5, COLS), f32)], axis=0)
    own = pltpu.roll(own, (COLS - tp * slim) % COLS, 1)
    for k, ref in enumerate((gw_ref, gm_ref, gv_ref)):
        ref[...] = own[k : k + 1, :slim]
    out_ref[KV + AVG :, :] = jnp.concatenate(
        [new[0][0], new[1][0], jnp.zeros((8 - NY, COLS), f32)], axis=0
    ).astype(bf16)


def final_kernel(tp_ref, got_ref, avg_ref, kv_ref, avg_out_ref, gain_ref):
    tp = tp_ref[0]
    for p in range(NY):
        for z in range(NZ):
            kv_ref[p, 0, z] = got_ref[0, z, p * ROWS : (p + 1) * ROWS, :]
            for k in range(NT):
                if k:
                    at = KV + (p * (NT - 1) + k - 1) * SL
                    new = got_ref[0, z, at : at + SL, :]
                else:
                    at = pl.multiple_of(p * ROWS + tp * SL, SL)
                    new = got_ref[0, z, pl.ds(at, SL), :]
                lanes = pl.ds(pl.multiple_of(((tp + k) % NT) * COLS, COLS), COLS)
                old = avg_ref[p, 0, z, :, lanes].astype(f32)
                avg_out_ref[p, 0, z, :, lanes] = (
                    0.8 * old + 0.2 * new.astype(f32)
                ).astype(bf16)
            gain_ref[p, 0, z : z + 1, :] = got_ref[0, z, KV + AVG + p : KV + AVG + p + 1, :]


def spread(block, axes, count):
    return lax.all_to_all(
        jnp.broadcast_to(block[None], (count,) + block.shape), axes, 0, 0, tiled=True
    )


def call(kernel, outs, *args, smem=0):
    specs = [pl.BlockSpec(memory_space=pltpu.SMEM)] * smem
    specs += [pl.BlockSpec(memory_space=pltpu.VMEM)] * (len(args) - smem)
    moved = sum(a.size * a.dtype.itemsize for a in args)
    return pl.pallas_call(
        kernel,
        out_shape=[jax.ShapeDtypeStruct(s, d) for s, d in outs],
        in_specs=specs,
        out_specs=[pl.BlockSpec(memory_space=pltpu.VMEM)] * len(outs),
        compiler_params=pltpu.CompilerParams(vmem_limit_bytes=8 << 20),
        cost_estimate=pl.CostEstimate(flops=moved, bytes_accessed=moved, transcendentals=0),
    )(*args)


def shards(
    grad_kv,
    grad_gains,
    kv_weight,
    kv_first,
    kv_second,
    gain_weight,
    gain_first,
    gain_second,
    average,
):
    yh = lax.axis_index("yh")
    tp = lax.axis_index(T)
    slim = gain_weight.shape[0]

    lanes = lax.broadcasted_iota(jnp.int32, (3, COLS), 1) // slim
    gains = jnp.tile(jnp.stack([gain_weight, gain_first, gain_second]), (1, NT))
    gains = jnp.where(lanes == tp, gains, 0.0)
    misc = jnp.concatenate([jnp.zeros((2, COLS), f32), gains, jnp.zeros((3, COLS), f32)])

    swap = [(0, 1), (1, 0)]
    peer_state = lax.ppermute(jnp.stack([kv_weight, kv_first, kv_second]), "yh", swap)

    count = NX * NZ
    sent = pl.pallas_call(
        pack_kernel,
        out_shape=jax.ShapeDtypeStruct((count, PACK, COLS), bf16),
        in_specs=[
            pl.BlockSpec(memory_space=pltpu.HBM),
            pl.BlockSpec(memory_space=pltpu.VMEM),
        ],
        out_specs=pl.BlockSpec(memory_space=pltpu.HBM),
        scratch_shapes=[
            pltpu.VMEM((count, 8, COLS), bf16),
            pltpu.SemaphoreType.DMA((NY * NX + 1,)),
        ],
    )(grad_kv.reshape(NY, count, ROWS, COLS), grad_gains.reshape(-1, COLS))
    got = lax.all_to_all(sent, ("x", "z"), 0, 0, tiled=True)
    got, peer_state = lax.optimization_barrier((got, peer_state))
    part, msg = call(
        sum_kernel,
        [((KV, COLS), f32), ((NY * NT, STATE + 3 * SL, COLS), f32)],
        got, misc, kv_weight, kv_first, kv_second,
    )
    peer = lax.ppermute(part, "yh", swap)

    got = lax.all_to_all(msg, ("yh",) + T, 0, 0, tiled=True)
    count = NX * NZ * NT
    rows, gain_rows, msg = call(
        norm_kernel,
        [((NY, NT, SL, COLS), f32), ((NY, 8, COLS), f32), ((count, COLS), f32)],
        got,
    )
    sums = lax.all_to_all(msg, ("x", "z") + T, 0, 0, tiled=True)

    kv_w, kv_m, kv_v, gain_w, gain_m, gain_v, block = call(
        update_kernel,
        [((ROWS, COLS), f32)] * 3 + [((1, slim), f32)] * 3 + [((BLOCK, COLS), bf16)],
        jnp.stack([yh, tp]).astype(jnp.int32),
        sums, part, peer, kv_weight, kv_first, kv_second, peer_state, rows, got, gain_rows,
        smem=1,
    )

    block = spread(block, "z", NZ)
    block = spread(block, "x", NX)

    def at_x(*shape):
        return pl.BlockSpec((NY, 1) + shape, lambda i: (0, i) + (0,) * len(shape))

    kv_blocks, average_out, gain_copy = pl.pallas_call(
        final_kernel,
        grid=(NX,),
        in_specs=[
            pl.BlockSpec(memory_space=pltpu.SMEM),
            pl.BlockSpec((1, NZ, BLOCK, COLS), lambda i: (i, 0, 0, 0)),
            at_x(NZ, SL, NT * COLS),
        ],
        out_specs=[at_x(NZ, ROWS, COLS), at_x(NZ, SL, NT * COLS), at_x(NZ, COLS)],
        out_shape=[
            jax.ShapeDtypeStruct((NY, NX, NZ, ROWS, COLS), bf16),
            jax.ShapeDtypeStruct((NY, NX, NZ, SL, NT * COLS), bf16),
            jax.ShapeDtypeStruct((NY, NX, NZ, COLS), bf16),
        ],
        compiler_params=pltpu.CompilerParams(vmem_limit_bytes=8 << 20),
    )(tp.astype(jnp.int32).reshape(1), block, average.reshape(NY, NX, NZ, SL, NT * COLS))
    return (
        kv_w, kv_m, kv_v, gain_w.reshape(-1), gain_m.reshape(-1), gain_v.reshape(-1),
        kv_blocks.reshape(-1, COLS), gain_copy.reshape(-1), average_out.reshape(average.shape),
    )


def solution(mesh):
    fine = Mesh(mesh.devices.reshape(NY, NX, NZ, 4, 2), F + T)
    in_specs = (
        P(F, None, T),
        P(F, T, None),
        P(F, T),
        P(F, T),
        P(F, T),
        P(F + T),
        P(F + T),
        P(F + T),
        P(None, T, None),
    )
    out_specs = (
        P(F, T),
        P(F, T),
        P(F, T),
        P(F + T),
        P(F + T),
        P(F + T),
        P(None, T),
        P(),
        P(None, T, None),
    )
    return jax.shard_map(shards, mesh=fine, in_specs=in_specs, out_specs=out_specs, check_vma=False)
```

```python
import jax
import jax.numpy as jnp
from jax import lax
from jax.experimental import pallas as pl
from jax.experimental.pallas import tpu as pltpu
from jax.sharding import Mesh, PartitionSpec as P

STEP = 100
PARAMS = 4202496
F = ("yh", "x", "z")
T = ("yl", "c")
NY, NX, NZ, NT = 2, 4, 8, 8
NF = NY * NX * NZ
ROWS, COLS = 64, 128
SL = ROWS // NT
PACK = ROWS + 8
STATE = SL + 8
MSG = STATE + 3 * SL
AVG = (NT - 1) * SL
BLOCK = ROWS + AVG + 8
f32, bf16 = jnp.float32, jnp.bfloat16


def adam_update(grad, first, second, weight, factor, decay):
    clipped = factor * grad
    first_new = 0.9 * first + 0.1 * clipped
    second_new = 0.95 * second + 0.05 * clipped * clipped
    first_fix = 1.0 - 0.9**STEP
    second_fix = 1.0 - 0.95**STEP
    step_dir = first_new / first_fix / (jnp.sqrt(second_new / second_fix) + 1e-08)
    weight_new = weight - 0.001 * (step_dir + decay * weight)
    return (weight_new, first_new, second_new)


def sum_kernel(got_ref, misc_ref, w_ref, m_ref, v_ref, part_ref, msg_ref):
    square = jnp.zeros((SL, COLS), f32)
    for r in range(0, PACK, SL):
        acc = got_ref[0, r : r + SL, :].astype(f32)
        for s in range(1, NF):
            acc += got_ref[s, r : r + SL, :].astype(f32)
        if r < ROWS:
            part_ref[r : r + SL, :] = acc
            msg_ref[r // SL, :SL, :] = acc
            square += acc * acc
    at = lax.broadcasted_iota(jnp.int32, (8, COLS), 0)
    line = jnp.broadcast_to(jnp.sum(square, axis=0, keepdims=True), (8, COLS))
    misc = jnp.where(at == 0, acc, jnp.where(at == 1, line, misc_ref[...]))
    for t in range(NT):
        msg_ref[t, SL:STATE, :] = misc
        for k, ref in enumerate((w_ref, m_ref, v_ref)):
            msg_ref[t, STATE + k * SL : STATE + (k + 1) * SL, :] = ref[t * SL : (t + 1) * SL, :]


def norm_kernel(got_ref, gain_ref, msg_ref):
    acc = got_ref[0, SL:STATE, :]
    for t in range(1, NT):
        acc += got_ref[t, SL:STATE, :]
    gain_ref[...] = acc
    line = acc[1:2] + acc[0:1] * acc[0:1]
    msg_ref[...] = jnp.broadcast_to(line, msg_ref.shape)


def update_kernel(
    tp_ref, sums_ref, part_ref, w0_ref, m0_ref, v0_ref, got_ref, gain_ref,
    w_ref, m_ref, v_ref, gw_ref, gm_ref, gv_ref, out_ref,
):
    total = jnp.sum(sums_ref[...])
    factor = jnp.minimum(
        f32(1.0), 1.0 / jnp.sqrt(jnp.full((1, COLS), total) / PARAMS + 1e-06)
    )
    tp = tp_ref[0]
    w, m, v = adam_update(
        part_ref[...], m0_ref[...], v0_ref[...], w0_ref[...], factor, 0.1
    )
    w_ref[...] = w
    m_ref[...] = m
    v_ref[...] = v
    out_ref[:ROWS, :] = w.astype(bf16)
    for k in range(1, NT):
        t = (tp + k) % NT
        old = [got_ref[t, STATE + j * SL : STATE + (j + 1) * SL, :] for j in range(3)]
        w, _, _ = adam_update(got_ref[t, :SL, :], old[1], old[2], old[0], factor, 0.1)
        at = ROWS + (k - 1) * SL
        out_ref[at : at + SL, :] = w.astype(bf16)
    rows = gain_ref[...]
    new = adam_update(rows[0:1], rows[3:4], rows[4:5], rows[2:3], factor, 0.0)
    slim = COLS // NT
    own = jnp.concatenate(list(new) + [jnp.zeros((5, COLS), f32)], axis=0)
    own = pltpu.roll(own, (COLS - tp * slim) % COLS, 1)
    for k, ref in enumerate((gw_ref, gm_ref, gv_ref)):
        ref[...] = own[k : k + 1, :slim]
    out_ref[ROWS + AVG :, :] = jnp.concatenate(
        [new[0], jnp.zeros((7, COLS), f32)], axis=0
    ).astype(bf16)


def final_kernel(tp_ref, got_ref, avg_ref, kv_ref, avg_out_ref, gain_ref):
    tp = tp_ref[0]
    for p in range(NY):
        for z in range(NZ):
            kv_ref[p, 0, z] = got_ref[0, p, z, :ROWS, :]
            for k in range(NT):
                if k:
                    at = ROWS + (k - 1) * SL
                    new = got_ref[0, p, z, at : at + SL, :]
                else:
                    new = got_ref[0, p, z, pl.ds(pl.multiple_of(tp * SL, SL), SL), :]
                lanes = pl.ds(pl.multiple_of(((tp + k) % NT) * COLS, COLS), COLS)
                old = avg_ref[p, 0, z, :, lanes].astype(f32)
                avg_out_ref[p, 0, z, :, lanes] = (
                    0.8 * old + 0.2 * new.astype(f32)
                ).astype(bf16)
            gain_ref[p, 0, z : z + 1, :] = got_ref[0, p, z, ROWS + AVG : ROWS + AVG + 1, :]


def spread(block, axes, count):
    return lax.all_to_all(
        jnp.broadcast_to(block[None], (count,) + block.shape), axes, 0, 0, tiled=True
    )


def call(kernel, outs, *args, smem=0):
    specs = [pl.BlockSpec(memory_space=pltpu.SMEM)] * smem
    specs += [pl.BlockSpec(memory_space=pltpu.VMEM)] * (len(args) - smem)
    moved = sum(a.size * a.dtype.itemsize for a in args)
    return pl.pallas_call(
        kernel,
        out_shape=[jax.ShapeDtypeStruct(s, d) for s, d in outs],
        in_specs=specs,
        out_specs=[pl.BlockSpec(memory_space=pltpu.VMEM)] * len(outs),
        compiler_params=pltpu.CompilerParams(vmem_limit_bytes=8 << 20),
        cost_estimate=pl.CostEstimate(flops=moved, bytes_accessed=moved, transcendentals=0),
    )(*args)


def shards(
    grad_kv,
    grad_gains,
    kv_weight,
    kv_first,
    kv_second,
    gain_weight,
    gain_first,
    gain_second,
    average,
):
    tp = lax.axis_index(T)
    slim = gain_weight.shape[0]
    at = tp.astype(jnp.int32).reshape(1)

    lanes = lax.broadcasted_iota(jnp.int32, (3, COLS), 1) // slim
    gains = jnp.tile(jnp.stack([gain_weight, gain_first, gain_second]), (1, NT))
    gains = jnp.where(lanes == tp, gains, 0.0)
    misc = jnp.concatenate([jnp.zeros((2, COLS), f32), gains, jnp.zeros((3, COLS), f32)])

    sent = jnp.concatenate(
        [
            grad_kv.reshape(NF, ROWS, COLS),
            grad_gains.reshape(NF, 1, COLS),
            jnp.zeros((NF, 7, COLS), bf16),
        ],
        axis=1,
    )
    sent, misc = lax.optimization_barrier((sent, misc))
    got = lax.all_to_all(sent, F, 0, 0, tiled=True)
    part, msg = call(
        sum_kernel,
        [((ROWS, COLS), f32), ((NT, MSG, COLS), f32)],
        got, misc, kv_weight, kv_first, kv_second,
    )

    got = lax.all_to_all(msg, T, 0, 0, tiled=True)
    gain_rows, msg = call(norm_kernel, [((8, COLS), f32), ((NF, COLS), f32)], got)
    sums = lax.all_to_all(msg, F, 0, 0, tiled=True)

    kv_w, kv_m, kv_v, gain_w, gain_m, gain_v, block = call(
        update_kernel,
        [((ROWS, COLS), f32)] * 3 + [((1, slim), f32)] * 3 + [((BLOCK, COLS), bf16)],
        at, sums, part, kv_weight, kv_first, kv_second, got, gain_rows,
        smem=1,
    )

    block = spread(block, ("yh", "z"), NY * NZ).reshape(NY, NZ, BLOCK, COLS)
    block = spread(block, "x", NX)

    def at_x(*shape):
        return pl.BlockSpec((NY, 1) + shape, lambda i: (0, i) + (0,) * len(shape))

    kv_blocks, average_out, gain_copy = pl.pallas_call(
        final_kernel,
        grid=(NX,),
        in_specs=[
            pl.BlockSpec(memory_space=pltpu.SMEM),
            pl.BlockSpec((1, NY, NZ, BLOCK, COLS), lambda i: (i, 0, 0, 0, 0)),
            at_x(NZ, SL, NT * COLS),
        ],
        out_specs=[at_x(NZ, ROWS, COLS), at_x(NZ, SL, NT * COLS), at_x(NZ, COLS)],
        out_shape=[
            jax.ShapeDtypeStruct((NY, NX, NZ, ROWS, COLS), bf16),
            jax.ShapeDtypeStruct((NY, NX, NZ, SL, NT * COLS), bf16),
            jax.ShapeDtypeStruct((NY, NX, NZ, COLS), bf16),
        ],
        compiler_params=pltpu.CompilerParams(vmem_limit_bytes=8 << 20),
    )(at, block, average.reshape(NY, NX, NZ, SL, NT * COLS))
    return (
        kv_w, kv_m, kv_v, gain_w.reshape(-1), gain_m.reshape(-1), gain_v.reshape(-1),
        kv_blocks.reshape(-1, COLS), gain_copy.reshape(-1), average_out.reshape(average.shape),
    )


def solution(mesh):
    fine = Mesh(mesh.devices.reshape(NY, NX, NZ, 4, 2), F + T)
    in_specs = (
        P(F, None, T),
        P(F, T, None),
        P(F, T),
        P(F, T),
        P(F, T),
        P(F + T),
        P(F + T),
        P(F + T),
        P(None, T, None),
    )
    out_specs = (
        P(F, T),
        P(F, T),
        P(F, T),
        P(F + T),
        P(F + T),
        P(F + T),
        P(None, T),
        P(),
        P(None, T, None),
    )
    return jax.shard_map(shards, mesh=fine, in_specs=in_specs, out_specs=out_specs, check_vma=False)
```

```python
import jax
import jax.numpy as jnp
from jax import lax
from jax.experimental import pallas as pl
from jax.experimental.pallas import tpu as pltpu
from jax.sharding import Mesh, PartitionSpec as P

STEP = 100
PARAMS = 4202496
F = ("yh", "x", "z")
T = ("yl", "c")
NY, NX, NZ, NT = 2, 4, 8, 8
NF = NY * NX * NZ
ROWS, COLS = 64, 128
SL = ROWS // NT
PACK = ROWS + 8
STATE = SL + 8
MSG = STATE + 3 * SL
AVG = (NT - 1) * SL
BLOCK = ROWS + AVG + 8
f32, bf16 = jnp.float32, jnp.bfloat16


def adam_update(grad, first, second, weight, factor, decay):
    clipped = factor * grad
    first_new = 0.9 * first + 0.1 * clipped
    second_new = 0.95 * second + 0.05 * clipped * clipped
    first_fix = 1.0 - 0.9**STEP
    second_fix = 1.0 - 0.95**STEP
    step_dir = first_new / first_fix / (jnp.sqrt(second_new / second_fix) + 1e-08)
    weight_new = weight - 0.001 * (step_dir + decay * weight)
    return (weight_new, first_new, second_new)


def sum_kernel(
    tp_ref, got_ref, gw_ref, gm_ref, gv_ref, w_ref, m_ref, v_ref, part_ref, msg_ref
):
    square = jnp.zeros((SL, COLS), f32)
    for r in range(0, PACK, SL):
        acc = got_ref[0, r : r + SL, :].astype(f32)
        for s in range(1, NF):
            acc += got_ref[s, r : r + SL, :].astype(f32)
        if r < ROWS:
            part_ref[r : r + SL, :] = acc
            msg_ref[r // SL, :SL, :] = acc
            square += acc * acc
    at = lax.broadcasted_iota(jnp.int32, (8, COLS), 0)
    line = jnp.broadcast_to(jnp.sum(square, axis=0, keepdims=True), (8, COLS))
    slim = COLS // NT
    gains = jnp.concatenate([ref[...] for ref in (gw_ref, gm_ref, gv_ref)], axis=0)
    gains = jnp.concatenate([gains, jnp.zeros((3, COLS - slim), f32)], axis=1)
    gains = jnp.concatenate([jnp.zeros((2, COLS), f32), gains, jnp.zeros((3, COLS), f32)])
    gains = pltpu.roll(gains, tp_ref[0] * slim, 1)
    misc = jnp.where(at == 0, acc, jnp.where(at == 1, line, gains))
    for t in range(NT):
        msg_ref[t, SL:STATE, :] = misc
        for k, ref in enumerate((w_ref, m_ref, v_ref)):
            msg_ref[t, STATE + k * SL : STATE + (k + 1) * SL, :] = ref[t * SL : (t + 1) * SL, :]


def norm_kernel(got_ref, gain_ref, msg_ref):
    acc = got_ref[0, SL:STATE, :]
    for t in range(1, NT):
        acc += got_ref[t, SL:STATE, :]
    gain_ref[...] = acc
    line = acc[1:2] + acc[0:1] * acc[0:1]
    msg_ref[...] = jnp.broadcast_to(line, msg_ref.shape)


def update_kernel(
    tp_ref, sums_ref, part_ref, w0_ref, m0_ref, v0_ref, got_ref, gain_ref,
    w_ref, m_ref, v_ref, gw_ref, gm_ref, gv_ref, out_ref,
):
    total = jnp.sum(sums_ref[...])
    factor = jnp.minimum(
        f32(1.0), 1.0 / jnp.sqrt(jnp.full((1, COLS), total) / PARAMS + 1e-06)
    )
    tp = tp_ref[0]
    w, m, v = adam_update(
        part_ref[...], m0_ref[...], v0_ref[...], w0_ref[...], factor, 0.1
    )
    w_ref[...] = w
    m_ref[...] = m
    v_ref[...] = v
    out_ref[:ROWS, :] = w.astype(bf16)
    for k in range(1, NT):
        t = (tp + k) % NT
        old = [got_ref[t, STATE + j * SL : STATE + (j + 1) * SL, :] for j in range(3)]
        w, _, _ = adam_update(got_ref[t, :SL, :], old[1], old[2], old[0], factor, 0.1)
        at = ROWS + (k - 1) * SL
        out_ref[at : at + SL, :] = w.astype(bf16)
    rows = gain_ref[...]
    new = adam_update(rows[0:1], rows[3:4], rows[4:5], rows[2:3], factor, 0.0)
    slim = COLS // NT
    own = jnp.concatenate(list(new) + [jnp.zeros((5, COLS), f32)], axis=0)
    own = pltpu.roll(own, (COLS - tp * slim) % COLS, 1)
    for k, ref in enumerate((gw_ref, gm_ref, gv_ref)):
        ref[...] = own[k : k + 1, :slim]
    out_ref[ROWS + AVG :, :] = jnp.concatenate(
        [new[0], jnp.zeros((7, COLS), f32)], axis=0
    ).astype(bf16)


def final_kernel(
    tp_ref, got_ref, avg_ref, kv_ref, avg_out_ref, gain_ref, blend_ref, kv_sems, avg_sems
):
    tp = tp_ref[0]

    def kv_copy(i):
        p, x = i // NX, i % NX
        return pltpu.make_async_copy(
            got_ref.at[x, p, :, pl.ds(0, ROWS)], kv_ref.at[p, x], kv_sems.at[i]
        )

    def avg_copy(i):
        p, x = i // NX, i % NX
        return pltpu.make_async_copy(blend_ref.at[p, x], avg_out_ref.at[p, x], avg_sems.at[i])

    for i in range(NY * NX):
        kv_copy(i).start()

    @pl.loop(0, NY * NX)
    def _(i):
        p, x = i // NX, i % NX
        for z in range(NZ):
            for k in range(NT):
                if k:
                    at = ROWS + (k - 1) * SL
                    new = got_ref[x, p, z, at : at + SL, :]
                else:
                    new = got_ref[x, p, z, pl.ds(pl.multiple_of(tp * SL, SL), SL), :]
                lanes = pl.ds(pl.multiple_of(((tp + k) % NT) * COLS, COLS), COLS)
                old = avg_ref[p, x, z, :, lanes].astype(f32)
                blend_ref[p, x, z, :, lanes] = (
                    0.8 * old + 0.2 * new.astype(f32)
                ).astype(bf16)
        avg_copy(i).start()

    for p in range(NY):
        for x in range(NX):
            for z in range(NZ):
                gain_ref[p, x, z : z + 1, :] = got_ref[
                    x, p, z, ROWS + AVG : ROWS + AVG + 1, :
                ]
    for i in range(NY * NX):
        kv_copy(i).wait()
        avg_copy(i).wait()


def spread(block, axes, count):
    return lax.all_to_all(
        jnp.broadcast_to(block[None], (count,) + block.shape), axes, 0, 0, tiled=True
    )


def call(kernel, outs, *args, smem=0):
    specs = [pl.BlockSpec(memory_space=pltpu.SMEM)] * smem
    specs += [pl.BlockSpec(memory_space=pltpu.VMEM)] * (len(args) - smem)
    moved = sum(a.size * a.dtype.itemsize for a in args)
    return pl.pallas_call(
        kernel,
        out_shape=[jax.ShapeDtypeStruct(s, d) for s, d in outs],
        in_specs=specs,
        out_specs=[pl.BlockSpec(memory_space=pltpu.VMEM)] * len(outs),
        compiler_params=pltpu.CompilerParams(vmem_limit_bytes=8 << 20),
        cost_estimate=pl.CostEstimate(flops=moved, bytes_accessed=moved, transcendentals=0),
    )(*args)


def shards(
    grad_kv,
    grad_gains,
    kv_weight,
    kv_first,
    kv_second,
    gain_weight,
    gain_first,
    gain_second,
    average,
):
    tp = lax.axis_index(T)
    slim = gain_weight.shape[0]
    at = tp.astype(jnp.int32).reshape(1)

    sent = jnp.concatenate(
        [
            grad_kv.reshape(NF, ROWS, COLS),
            grad_gains.reshape(NF, 1, COLS),
            jnp.zeros((NF, 7, COLS), bf16),
        ],
        axis=1,
    )
    sent, at = lax.optimization_barrier((sent, at))
    got = lax.all_to_all(sent, F, 0, 0, tiled=True)
    part, msg = call(
        sum_kernel,
        [((ROWS, COLS), f32), ((NT, MSG, COLS), f32)],
        at, got,
        gain_weight.reshape(1, slim), gain_first.reshape(1, slim), gain_second.reshape(1, slim),
        kv_weight, kv_first, kv_second,
        smem=1,
    )

    got = lax.all_to_all(msg, T, 0, 0, tiled=True)
    gain_rows, msg = call(norm_kernel, [((8, COLS), f32), ((NF, COLS), f32)], got)
    sums = lax.all_to_all(msg, F, 0, 0, tiled=True)

    kv_w, kv_m, kv_v, gain_w, gain_m, gain_v, block = call(
        update_kernel,
        [((ROWS, COLS), f32)] * 3 + [((1, slim), f32)] * 3 + [((BLOCK, COLS), bf16)],
        at, sums, part, kv_weight, kv_first, kv_second, got, gain_rows,
        smem=1,
    )

    block = spread(block, ("yh", "z"), NY * NZ).reshape(NY, NZ, BLOCK, COLS)
    block = spread(block, "x", NX)

    vmem, hbm = pl.BlockSpec(memory_space=pltpu.VMEM), pl.BlockSpec(memory_space=pltpu.HBM)
    kv_blocks, average_out, gain_copy = pl.pallas_call(
        final_kernel,
        in_specs=[pl.BlockSpec(memory_space=pltpu.SMEM), vmem, vmem],
        out_specs=[hbm, hbm, vmem],
        out_shape=[
            jax.ShapeDtypeStruct((NY, NX, NZ, ROWS, COLS), bf16),
            jax.ShapeDtypeStruct((NY, NX, NZ, SL, NT * COLS), bf16),
            jax.ShapeDtypeStruct((NY, NX, NZ, COLS), bf16),
        ],
        scratch_shapes=[
            pltpu.VMEM((NY, NX, NZ, SL, NT * COLS), bf16),
            pltpu.SemaphoreType.DMA((NY * NX,)),
            pltpu.SemaphoreType.DMA((NY * NX,)),
        ],
        compiler_params=pltpu.CompilerParams(vmem_limit_bytes=8 << 20),
    )(at, block, average.reshape(NY, NX, NZ, SL, NT * COLS))
    return (
        kv_w, kv_m, kv_v, gain_w.reshape(-1), gain_m.reshape(-1), gain_v.reshape(-1),
        kv_blocks.reshape(-1, COLS), gain_copy.reshape(-1), average_out.reshape(average.shape),
    )


def solution(mesh):
    fine = Mesh(mesh.devices.reshape(NY, NX, NZ, 4, 2), F + T)
    in_specs = (
        P(F, None, T),
        P(F, T, None),
        P(F, T),
        P(F, T),
        P(F, T),
        P(F + T),
        P(F + T),
        P(F + T),
        P(None, T, None),
    )
    out_specs = (
        P(F, T),
        P(F, T),
        P(F, T),
        P(F + T),
        P(F + T),
        P(F + T),
        P(None, T),
        P(),
        P(None, T, None),
    )
    return jax.shard_map(shards, mesh=fine, in_specs=in_specs, out_specs=out_specs, check_vma=False)
```

```python
import jax
import jax.numpy as jnp
from jax import lax
from jax.experimental import pallas as pl
from jax.experimental.pallas import tpu as pltpu
from jax.sharding import Mesh, PartitionSpec as P

STEP = 100
PARAMS = 4202496
F = ("yh", "x", "z")
T = ("yl", "c")
NY, NX, NZ, NT = 2, 4, 8, 8
NF = NY * NX * NZ
ROWS, COLS = 64, 128
SL = ROWS // NT
PACK = ROWS + 8
STATE = SL + 8
MSG = STATE + 3 * SL
AVG = (NT - 1) * SL
BLOCK = ROWS + AVG + 8
f32, bf16 = jnp.float32, jnp.bfloat16


def adam_update(grad, first, second, weight, factor, decay):
    clipped = factor * grad
    first_new = 0.9 * first + 0.1 * clipped
    second_new = 0.95 * second + 0.05 * clipped * clipped
    first_fix = 1.0 - 0.9**STEP
    second_fix = 1.0 - 0.95**STEP
    step_dir = first_new / first_fix / (jnp.sqrt(second_new / second_fix) + 1e-08)
    weight_new = weight - 0.001 * (step_dir + decay * weight)
    return (weight_new, first_new, second_new)


def pack_kernel(grad_ref, gain_ref, out_ref, sems):
    size = NF // 8
    copies = [
        pltpu.make_async_copy(
            grad_ref.at[pl.ds(i * size, size)],
            out_ref.at[pl.ds(i * size, size), pl.ds(0, ROWS)],
            sems.at[i],
        )
        for i in range(8)
    ]
    for copy in copies:
        copy.start()
    zero = jnp.zeros((7, COLS), f32)
    for d in range(NF):
        tail = jnp.concatenate([gain_ref[d].astype(f32), zero], axis=0)
        out_ref[d, ROWS:, :] = tail.astype(bf16)
    for copy in copies:
        copy.wait()


def sum_kernel(
    tp_ref, got_ref, gw_ref, gm_ref, gv_ref, w_ref, m_ref, v_ref, part_ref, msg_ref
):
    square = jnp.zeros((SL, COLS), f32)
    for r in range(0, PACK, SL):
        acc = got_ref[0, r : r + SL, :].astype(f32)
        for s in range(1, NF):
            acc += got_ref[s, r : r + SL, :].astype(f32)
        if r < ROWS:
            part_ref[r : r + SL, :] = acc
            msg_ref[r // SL, :SL, :] = acc
            square += acc * acc
    at = lax.broadcasted_iota(jnp.int32, (8, COLS), 0)
    line = jnp.broadcast_to(jnp.sum(square, axis=0, keepdims=True), (8, COLS))
    slim = COLS // NT
    gains = jnp.concatenate([ref[...] for ref in (gw_ref, gm_ref, gv_ref)], axis=0)
    gains = jnp.concatenate([gains, jnp.zeros((3, COLS - slim), f32)], axis=1)
    gains = jnp.concatenate([jnp.zeros((2, COLS), f32), gains, jnp.zeros((3, COLS), f32)])
    gains = pltpu.roll(gains, tp_ref[0] * slim, 1)
    misc = jnp.where(at == 0, acc, jnp.where(at == 1, line, gains))
    for t in range(NT):
        msg_ref[t, SL:STATE, :] = misc
        for k, ref in enumerate((w_ref, m_ref, v_ref)):
            msg_ref[t, STATE + k * SL : STATE + (k + 1) * SL, :] = ref[t * SL : (t + 1) * SL, :]


def norm_kernel(got_ref, gain_ref, msg_ref):
    acc = got_ref[0, SL:STATE, :]
    for t in range(1, NT):
        acc += got_ref[t, SL:STATE, :]
    gain_ref[...] = acc
    line = acc[1:2] + acc[0:1] * acc[0:1]
    msg_ref[...] = jnp.broadcast_to(line, msg_ref.shape)


def update_kernel(
    tp_ref, sums_ref, part_ref, w0_ref, m0_ref, v0_ref, got_ref, gain_ref,
    w_ref, m_ref, v_ref, gw_ref, gm_ref, gv_ref, out_ref,
):
    total = jnp.sum(sums_ref[...])
    factor = jnp.minimum(
        f32(1.0), 1.0 / jnp.sqrt(jnp.full((1, COLS), total) / PARAMS + 1e-06)
    )
    tp = tp_ref[0]
    w, m, v = adam_update(
        part_ref[...], m0_ref[...], v0_ref[...], w0_ref[...], factor, 0.1
    )
    w_ref[...] = w
    m_ref[...] = m
    v_ref[...] = v
    out_ref[:ROWS, :] = w.astype(bf16)
    for k in range(1, NT):
        t = (tp + k) % NT
        old = [got_ref[t, STATE + j * SL : STATE + (j + 1) * SL, :] for j in range(3)]
        w, _, _ = adam_update(got_ref[t, :SL, :], old[1], old[2], old[0], factor, 0.1)
        at = ROWS + (k - 1) * SL
        out_ref[at : at + SL, :] = w.astype(bf16)
    rows = gain_ref[...]
    new = adam_update(rows[0:1], rows[3:4], rows[4:5], rows[2:3], factor, 0.0)
    slim = COLS // NT
    own = jnp.concatenate(list(new) + [jnp.zeros((5, COLS), f32)], axis=0)
    own = pltpu.roll(own, (COLS - tp * slim) % COLS, 1)
    for k, ref in enumerate((gw_ref, gm_ref, gv_ref)):
        ref[...] = own[k : k + 1, :slim]
    out_ref[ROWS + AVG :, :] = jnp.concatenate(
        [new[0], jnp.zeros((7, COLS), f32)], axis=0
    ).astype(bf16)


def final_kernel(
    tp_ref, got_ref, avg_ref, kv_ref, avg_out_ref, gain_ref, blend_ref, kv_sems, avg_sems
):
    tp = tp_ref[0]

    def kv_copy(i):
        p, x = i // NX, i % NX
        return pltpu.make_async_copy(
            got_ref.at[x, p, :, pl.ds(0, ROWS)], kv_ref.at[p, x], kv_sems.at[i]
        )

    def avg_copy(i):
        p, x = i // NX, i % NX
        return pltpu.make_async_copy(blend_ref.at[p, x], avg_out_ref.at[p, x], avg_sems.at[i])

    for i in range(NY * NX):
        kv_copy(i).start()

    starts = []
    for t in range(NT):
        k = (t + NT - tp) % NT
        start = jnp.where(k == 0, tp * SL, ROWS + (k - 1) * SL)
        starts.append(pl.multiple_of(start, SL))

    @pl.loop(0, NY * NX)
    def _(i):
        p, x = i // NX, i % NX
        for z in range(NZ):
            for t in range(NT):
                lanes = slice(t * COLS, (t + 1) * COLS)
                new = got_ref[x, p, z, pl.ds(starts[t], SL), :].astype(f32)
                old = avg_ref[p, x, z, :, lanes].astype(f32)
                blend_ref[p, x, z, :, lanes] = (0.8 * old + 0.2 * new).astype(bf16)
        avg_copy(i).start()

    for p in range(NY):
        for x in range(NX):
            for z in range(NZ):
                gain_ref[p, x, z : z + 1, :] = got_ref[
                    x, p, z, ROWS + AVG : ROWS + AVG + 1, :
                ]
    for i in range(NY * NX):
        kv_copy(i).wait()
        avg_copy(i).wait()


def spread(block, axes, count):
    return lax.all_to_all(
        jnp.broadcast_to(block[None], (count,) + block.shape), axes, 0, 0, tiled=True
    )


def call(kernel, outs, *args, smem=0):
    specs = [pl.BlockSpec(memory_space=pltpu.SMEM)] * smem
    specs += [pl.BlockSpec(memory_space=pltpu.VMEM)] * (len(args) - smem)
    moved = sum(a.size * a.dtype.itemsize for a in args)
    return pl.pallas_call(
        kernel,
        out_shape=[jax.ShapeDtypeStruct(s, d) for s, d in outs],
        in_specs=specs,
        out_specs=[pl.BlockSpec(memory_space=pltpu.VMEM)] * len(outs),
        compiler_params=pltpu.CompilerParams(vmem_limit_bytes=8 << 20),
        cost_estimate=pl.CostEstimate(flops=moved, bytes_accessed=moved, transcendentals=0),
    )(*args)


def shards(
    grad_kv,
    grad_gains,
    kv_weight,
    kv_first,
    kv_second,
    gain_weight,
    gain_first,
    gain_second,
    average,
):
    tp = lax.axis_index(T)
    slim = gain_weight.shape[0]
    at = tp.astype(jnp.int32).reshape(1)

    grads = pltpu.with_memory_space_constraint(
        grad_kv.reshape(NF, ROWS, COLS), pltpu.HBM
    )
    sent = pl.pallas_call(
        pack_kernel,
        out_shape=jax.ShapeDtypeStruct((NF, PACK, COLS), bf16),
        in_specs=[
            pl.BlockSpec(memory_space=pltpu.HBM),
            pl.BlockSpec(memory_space=pltpu.VMEM),
        ],
        out_specs=pl.BlockSpec(memory_space=pltpu.VMEM),
        scratch_shapes=[pltpu.SemaphoreType.DMA((8,))],
        compiler_params=pltpu.CompilerParams(vmem_limit_bytes=8 << 20),
    )(grads, grad_gains.reshape(NF, 1, COLS))
    sent, at = lax.optimization_barrier((sent, at))
    got = lax.all_to_all(sent, F, 0, 0, tiled=True)
    part, msg = call(
        sum_kernel,
        [((ROWS, COLS), f32), ((NT, MSG, COLS), f32)],
        at, got,
        gain_weight.reshape(1, slim), gain_first.reshape(1, slim), gain_second.reshape(1, slim),
        kv_weight, kv_first, kv_second,
        smem=1,
    )

    got = lax.all_to_all(msg, T, 0, 0, tiled=True)
    gain_rows, msg = call(norm_kernel, [((8, COLS), f32), ((NF, COLS), f32)], got)
    sums = lax.all_to_all(msg, F, 0, 0, tiled=True)

    kv_w, kv_m, kv_v, gain_w, gain_m, gain_v, block = call(
        update_kernel,
        [((ROWS, COLS), f32)] * 3 + [((1, slim), f32)] * 3 + [((BLOCK, COLS), bf16)],
        at, sums, part, kv_weight, kv_first, kv_second, got, gain_rows,
        smem=1,
    )

    block = spread(block, ("yh", "z"), NY * NZ).reshape(NY, NZ, BLOCK, COLS)
    block = spread(block, "x", NX)

    vmem, hbm = pl.BlockSpec(memory_space=pltpu.VMEM), pl.BlockSpec(memory_space=pltpu.HBM)
    kv_blocks, average_out, gain_copy = pl.pallas_call(
        final_kernel,
        in_specs=[pl.BlockSpec(memory_space=pltpu.SMEM), vmem, vmem],
        out_specs=[hbm, hbm, vmem],
        out_shape=[
            jax.ShapeDtypeStruct((NY, NX, NZ, ROWS, COLS), bf16),
            jax.ShapeDtypeStruct((NY, NX, NZ, SL, NT * COLS), bf16),
            jax.ShapeDtypeStruct((NY, NX, NZ, COLS), bf16),
        ],
        scratch_shapes=[
            pltpu.VMEM((NY, NX, NZ, SL, NT * COLS), bf16),
            pltpu.SemaphoreType.DMA((NY * NX,)),
            pltpu.SemaphoreType.DMA((NY * NX,)),
        ],
        compiler_params=pltpu.CompilerParams(vmem_limit_bytes=8 << 20),
    )(at, block, average.reshape(NY, NX, NZ, SL, NT * COLS))
    return (
        kv_w, kv_m, kv_v, gain_w.reshape(-1), gain_m.reshape(-1), gain_v.reshape(-1),
        kv_blocks.reshape(-1, COLS), gain_copy.reshape(-1), average_out.reshape(average.shape),
    )


def solution(mesh):
    fine = Mesh(mesh.devices.reshape(NY, NX, NZ, 4, 2), F + T)
    in_specs = (
        P(F, None, T),
        P(F, T, None),
        P(F, T),
        P(F, T),
        P(F, T),
        P(F + T),
        P(F + T),
        P(F + T),
        P(None, T, None),
    )
    out_specs = (
        P(F, T),
        P(F, T),
        P(F, T),
        P(F + T),
        P(F + T),
        P(F + T),
        P(None, T),
        P(),
        P(None, T, None),
    )
    return jax.shard_map(shards, mesh=fine, in_specs=in_specs, out_specs=out_specs, check_vma=False)
```

```python
import jax
import jax.numpy as jnp
from jax import lax
from jax.experimental import pallas as pl
from jax.experimental.pallas import tpu as pltpu
from jax.sharding import Mesh, PartitionSpec as P

STEP = 100
PARAMS = 4202496
F = ("yh", "x", "z")
T = ("yl", "c")
NY, NX, NZ, NT = 2, 4, 8, 8
NF = NY * NX * NZ
ROWS, COLS = 64, 128
SL = ROWS // NT
PACK = ROWS + 8
STATE = SL + 8
MSG = STATE + 3 * SL
AVG = (NT - 1) * SL
BLOCK = ROWS + AVG + 8
f32, bf16 = jnp.float32, jnp.bfloat16


def adam_update(grad, first, second, weight, factor, decay):
    clipped = factor * grad
    first_new = 0.9 * first + 0.1 * clipped
    second_new = 0.95 * second + 0.05 * clipped * clipped
    first_fix = 1.0 - 0.9**STEP
    second_fix = 1.0 - 0.95**STEP
    step_dir = first_new / first_fix / (jnp.sqrt(second_new / second_fix) + 1e-08)
    weight_new = weight - 0.001 * (step_dir + decay * weight)
    return (weight_new, first_new, second_new)


def sum_kernel(
    tp_ref, got_ref, gw_ref, gm_ref, gv_ref, w_ref, m_ref, v_ref, part_ref, msg_ref
):
    square = jnp.zeros((SL, COLS), f32)
    for r in range(0, PACK, SL):
        acc = got_ref[0, r : r + SL, :].astype(f32)
        for s in range(1, NF):
            acc += got_ref[s, r : r + SL, :].astype(f32)
        if r < ROWS:
            part_ref[r : r + SL, :] = acc
            msg_ref[r // SL, :SL, :] = acc
            square += acc * acc
    at = lax.broadcasted_iota(jnp.int32, (8, COLS), 0)
    line = jnp.broadcast_to(jnp.sum(square, axis=0, keepdims=True), (8, COLS))
    slim = COLS // NT
    gains = jnp.concatenate([ref[...] for ref in (gw_ref, gm_ref, gv_ref)], axis=0)
    gains = jnp.concatenate([gains, jnp.zeros((3, COLS - slim), f32)], axis=1)
    gains = jnp.concatenate([jnp.zeros((2, COLS), f32), gains, jnp.zeros((3, COLS), f32)])
    gains = pltpu.roll(gains, tp_ref[0] * slim, 1)
    misc = jnp.where(at == 0, acc, jnp.where(at == 1, line, gains))
    for t in range(NT):
        msg_ref[t, SL:STATE, :] = misc
        for k, ref in enumerate((w_ref, m_ref, v_ref)):
            msg_ref[t, STATE + k * SL : STATE + (k + 1) * SL, :] = ref[t * SL : (t + 1) * SL, :]


def norm_kernel(got_ref, gain_ref, msg_ref):
    acc = got_ref[0, SL:STATE, :]
    for t in range(1, NT):
        acc += got_ref[t, SL:STATE, :]
    gain_ref[...] = acc
    line = acc[1:2] + acc[0:1] * acc[0:1]
    msg_ref[...] = jnp.broadcast_to(line, msg_ref.shape)


def update_kernel(
    tp_ref, sums_ref, part_ref, w0_ref, m0_ref, v0_ref, got_ref, gain_ref,
    w_ref, m_ref, v_ref, gw_ref, gm_ref, gv_ref, out_ref,
):
    total = jnp.sum(sums_ref[...])
    factor = jnp.minimum(
        f32(1.0), 1.0 / jnp.sqrt(jnp.full((1, COLS), total) / PARAMS + 1e-06)
    )
    tp = tp_ref[0]
    w, m, v = adam_update(
        part_ref[...], m0_ref[...], v0_ref[...], w0_ref[...], factor, 0.1
    )
    w_ref[...] = w
    m_ref[...] = m
    v_ref[...] = v
    out_ref[:ROWS, :] = w.astype(bf16)
    for k in range(1, NT):
        t = (tp + k) % NT
        old = [got_ref[t, STATE + j * SL : STATE + (j + 1) * SL, :] for j in range(3)]
        w, _, _ = adam_update(got_ref[t, :SL, :], old[1], old[2], old[0], factor, 0.1)
        at = ROWS + (k - 1) * SL
        out_ref[at : at + SL, :] = w.astype(bf16)
    rows = gain_ref[...]
    new = adam_update(rows[0:1], rows[3:4], rows[4:5], rows[2:3], factor, 0.0)
    slim = COLS // NT
    own = jnp.concatenate(list(new) + [jnp.zeros((5, COLS), f32)], axis=0)
    own = pltpu.roll(own, (COLS - tp * slim) % COLS, 1)
    for k, ref in enumerate((gw_ref, gm_ref, gv_ref)):
        ref[...] = own[k : k + 1, :slim]
    out_ref[ROWS + AVG :, :] = jnp.concatenate(
        [new[0], jnp.zeros((7, COLS), f32)], axis=0
    ).astype(bf16)


def final_kernel(
    at_ref, own_ref, r0_ref, r1_ref, d0_ref, d1_ref, l0_ref, l1_ref, avg_ref,
    kv_ref, avg_out_ref, gain_ref, blend_ref, kv_sems, avg_sems,
):
    tp, me = at_ref[0], at_ref[1]
    blocks = [
        [own_ref.at[0], r0_ref, d0_ref, l0_ref],
        [own_ref.at[1], r1_ref, d1_ref, l1_ref],
    ]
    places = [(p, ahead, (me + ahead) % NX) for p in range(NY) for ahead in range(NX)]
    copies = []
    for i, (p, ahead, x) in enumerate(places):
        copies.append(
            pltpu.make_async_copy(
                blocks[p][ahead].at[:, pl.ds(0, ROWS)], kv_ref.at[p, x], kv_sems.at[i]
            )
        )
        copies[-1].start()
    for i, (p, ahead, x) in enumerate(places):
        got_ref = blocks[p][ahead]

        @pl.loop(0, NZ)
        def _(z):
            for k in range(NT):
                if k:
                    at = ROWS + (k - 1) * SL
                    new = got_ref[z, at : at + SL, :]
                else:
                    new = got_ref[z, pl.ds(pl.multiple_of(tp * SL, SL), SL), :]
                lanes = pl.ds(pl.multiple_of(((tp + k) % NT) * COLS, COLS), COLS)
                old = avg_ref[p, x, z, :, lanes].astype(f32)
                blend_ref[p, ahead, z, :, lanes] = (
                    0.8 * old + 0.2 * new.astype(f32)
                ).astype(bf16)

        copies.append(
            pltpu.make_async_copy(
                blend_ref.at[p, ahead], avg_out_ref.at[p, x], avg_sems.at[i]
            )
        )
        copies[-1].start()
        rows = [
            got_ref[z, ROWS + AVG : ROWS + AVG + 1, :].astype(f32) for z in range(NZ)
        ]
        gain_ref[p, x] = jnp.concatenate(rows, axis=0).astype(bf16)
    for copy in copies:
        copy.wait()


def spread(block, axes, count):
    return lax.all_to_all(
        jnp.broadcast_to(block[None], (count,) + block.shape), axes, 0, 0, tiled=True
    )


def call(kernel, outs, *args, smem=0):
    specs = [pl.BlockSpec(memory_space=pltpu.SMEM)] * smem
    specs += [pl.BlockSpec(memory_space=pltpu.VMEM)] * (len(args) - smem)
    moved = sum(a.size * a.dtype.itemsize for a in args)
    return pl.pallas_call(
        kernel,
        out_shape=[jax.ShapeDtypeStruct(s, d) for s, d in outs],
        in_specs=specs,
        out_specs=[pl.BlockSpec(memory_space=pltpu.VMEM)] * len(outs),
        compiler_params=pltpu.CompilerParams(vmem_limit_bytes=8 << 20),
        cost_estimate=pl.CostEstimate(flops=moved, bytes_accessed=moved, transcendentals=0),
    )(*args)


def shards(
    grad_kv,
    grad_gains,
    kv_weight,
    kv_first,
    kv_second,
    gain_weight,
    gain_first,
    gain_second,
    average,
):
    tp = lax.axis_index(T)
    slim = gain_weight.shape[0]
    at = jnp.stack([tp, lax.axis_index("x")]).astype(jnp.int32)

    sent = jnp.concatenate(
        [
            grad_kv.reshape(NF, ROWS, COLS),
            grad_gains.reshape(NF, 1, COLS),
            jnp.zeros((NF, 7, COLS), bf16),
        ],
        axis=1,
    )
    sent, at = lax.optimization_barrier((sent, at))
    got = lax.all_to_all(sent, F, 0, 0, tiled=True)
    part, msg = call(
        sum_kernel,
        [((ROWS, COLS), f32), ((NT, MSG, COLS), f32)],
        at, got,
        gain_weight.reshape(1, slim), gain_first.reshape(1, slim), gain_second.reshape(1, slim),
        kv_weight, kv_first, kv_second,
        smem=1,
    )

    got = lax.all_to_all(msg, T, 0, 0, tiled=True)
    gain_rows, msg = call(norm_kernel, [((8, COLS), f32), ((NF, COLS), f32)], got)
    sums = lax.all_to_all(msg, F, 0, 0, tiled=True)

    kv_w, kv_m, kv_v, gain_w, gain_m, gain_v, block = call(
        update_kernel,
        [((ROWS, COLS), f32)] * 3 + [((1, slim), f32)] * 3 + [((BLOCK, COLS), bf16)],
        at, sums, part, kv_weight, kv_first, kv_second, got, gain_rows,
        smem=1,
    )

    block = spread(block, ("yh", "z"), NY * NZ).reshape(NY, NZ, BLOCK, COLS)
    ahead = [(i, (i + 1) % NX) for i in range(NX)]
    back = [(i, (i - 1) % NX) for i in range(NX)]
    half0, half1 = block[0], block[1]
    l0 = lax.ppermute(half0, "x", ahead)
    r1 = lax.ppermute(half1, "x", back)
    l1 = lax.ppermute(half1, "x", ahead)
    r0 = lax.ppermute(half0, "x", back)
    d0 = lax.ppermute(l0, "x", ahead)
    d1 = lax.ppermute(r1, "x", back)

    vmem, hbm = pl.BlockSpec(memory_space=pltpu.VMEM), pl.BlockSpec(memory_space=pltpu.HBM)
    kv_blocks, average_out, gain_copy = pl.pallas_call(
        final_kernel,
        in_specs=[pl.BlockSpec(memory_space=pltpu.SMEM)] + [vmem] * 8,
        out_specs=[hbm, hbm, vmem],
        out_shape=[
            jax.ShapeDtypeStruct((NY, NX, NZ, ROWS, COLS), bf16),
            jax.ShapeDtypeStruct((NY, NX, NZ, SL, NT * COLS), bf16),
            jax.ShapeDtypeStruct((NY, NX, NZ, COLS), bf16),
        ],
        scratch_shapes=[
            pltpu.VMEM((NY, NX, NZ, SL, NT * COLS), bf16),
            pltpu.SemaphoreType.DMA((NY * NX,)),
            pltpu.SemaphoreType.DMA((NY * NX,)),
        ],
        compiler_params=pltpu.CompilerParams(vmem_limit_bytes=8 << 20),
    )(at, block, r0, r1, d0, d1, l0, l1, average.reshape(NY, NX, NZ, SL, NT * COLS))
    return (
        kv_w, kv_m, kv_v, gain_w.reshape(-1), gain_m.reshape(-1), gain_v.reshape(-1),
        kv_blocks.reshape(-1, COLS), gain_copy.reshape(-1), average_out.reshape(average.shape),
    )


def solution(mesh):
    fine = Mesh(mesh.devices.reshape(NY, NX, NZ, 4, 2), F + T)
    in_specs = (
        P(F, None, T),
        P(F, T, None),
        P(F, T),
        P(F, T),
        P(F, T),
        P(F + T),
        P(F + T),
        P(F + T),
        P(None, T, None),
    )
    out_specs = (
        P(F, T),
        P(F, T),
        P(F, T),
        P(F + T),
        P(F + T),
        P(F + T),
        P(None, T),
        P(),
        P(None, T, None),
    )
    return jax.shard_map(shards, mesh=fine, in_specs=in_specs, out_specs=out_specs, check_vma=False)
```

```python
import functools

import jax
import jax.numpy as jnp
from jax import lax
from jax.experimental import pallas as pl
from jax.experimental.pallas import tpu as pltpu
from jax.sharding import Mesh, PartitionSpec as P

STEP = 100
PARAMS = 4202496
F = ("yh", "x", "z")
T = ("yl", "c")
NY, NX, NZ, NT = 2, 4, 8, 8
NF = NY * NX * NZ
ROWS, COLS = 64, 128
SL = ROWS // NT
PACK = ROWS + 8
STATE = SL + 8
MSG = STATE + 3 * SL
AVG = (NT - 1) * SL
BLOCK = ROWS + AVG + 8
f32, bf16 = jnp.float32, jnp.bfloat16


def adam_update(grad, first, second, weight, factor, decay):
    clipped = factor * grad
    first_new = 0.9 * first + 0.1 * clipped
    second_new = 0.95 * second + 0.05 * clipped * clipped
    first_fix = 1.0 - 0.9**STEP
    second_fix = 1.0 - 0.95**STEP
    step_dir = first_new / first_fix / (jnp.sqrt(second_new / second_fix) + 1e-08)
    weight_new = weight - 0.001 * (step_dir + decay * weight)
    return (weight_new, first_new, second_new)


def sum_kernel(
    tp_ref, got_ref, gw_ref, gm_ref, gv_ref, w_ref, m_ref, v_ref, part_ref, msg_ref
):
    square = jnp.zeros((SL, COLS), f32)
    for r in range(0, PACK, SL):
        acc = got_ref[0, r : r + SL, :].astype(f32)
        for s in range(1, NF):
            acc += got_ref[s, r : r + SL, :].astype(f32)
        if r < ROWS:
            part_ref[r : r + SL, :] = acc
            msg_ref[r // SL, :SL, :] = acc
            square += acc * acc
    at = lax.broadcasted_iota(jnp.int32, (8, COLS), 0)
    line = jnp.broadcast_to(jnp.sum(square, axis=0, keepdims=True), (8, COLS))
    slim = COLS // NT
    gains = jnp.concatenate([ref[...] for ref in (gw_ref, gm_ref, gv_ref)], axis=0)
    gains = jnp.concatenate([gains, jnp.zeros((3, COLS - slim), f32)], axis=1)
    gains = jnp.concatenate([jnp.zeros((2, COLS), f32), gains, jnp.zeros((3, COLS), f32)])
    gains = pltpu.roll(gains, tp_ref[0] * slim, 1)
    misc = jnp.where(at == 0, acc, jnp.where(at == 1, line, gains))
    for t in range(NT):
        msg_ref[t, SL:STATE, :] = misc
        for k, ref in enumerate((w_ref, m_ref, v_ref)):
            msg_ref[t, STATE + k * SL : STATE + (k + 1) * SL, :] = ref[t * SL : (t + 1) * SL, :]


def norm_kernel(got_ref, gain_ref, msg_ref):
    acc = got_ref[0, SL:STATE, :]
    for t in range(1, NT):
        acc += got_ref[t, SL:STATE, :]
    gain_ref[...] = acc
    line = acc[1:2] + acc[0:1] * acc[0:1]
    msg_ref[...] = jnp.broadcast_to(line, msg_ref.shape)


def update_kernel(
    tp_ref, sums_ref, part_ref, w0_ref, m0_ref, v0_ref, got_ref, gain_ref,
    w_ref, m_ref, v_ref, gw_ref, gm_ref, gv_ref, out_ref,
):
    total = jnp.sum(sums_ref[...])
    factor = jnp.minimum(
        f32(1.0), 1.0 / jnp.sqrt(jnp.full((1, COLS), total) / PARAMS + 1e-06)
    )
    tp = tp_ref[0]
    w, m, v = adam_update(
        part_ref[...], m0_ref[...], v0_ref[...], w0_ref[...], factor, 0.1
    )
    w_ref[...] = w
    m_ref[...] = m
    v_ref[...] = v
    out_ref[:ROWS, :] = w.astype(bf16)
    for k in range(1, NT):
        t = (tp + k) % NT
        old = [got_ref[t, STATE + j * SL : STATE + (j + 1) * SL, :] for j in range(3)]
        w, _, _ = adam_update(got_ref[t, :SL, :], old[1], old[2], old[0], factor, 0.1)
        at = ROWS + (k - 1) * SL
        out_ref[at : at + SL, :] = w.astype(bf16)
    rows = gain_ref[...]
    new = adam_update(rows[0:1], rows[3:4], rows[4:5], rows[2:3], factor, 0.0)
    slim = COLS // NT
    own = jnp.concatenate(list(new) + [jnp.zeros((5, COLS), f32)], axis=0)
    own = pltpu.roll(own, (COLS - tp * slim) % COLS, 1)
    for k, ref in enumerate((gw_ref, gm_ref, gv_ref)):
        ref[...] = own[k : k + 1, :slim]
    out_ref[ROWS + AVG :, :] = jnp.concatenate(
        [new[0], jnp.zeros((7, COLS), f32)], axis=0
    ).astype(bf16)


def place_kernel(parts, tp_ref, x_ref, avg_ref, *refs):
    count = len(parts)
    blocks = refs[:count]
    kv_ref, avg_out_ref, gain_ref, blend_ref, lines_ref, sems = refs[-6:]
    tp, me = tp_ref[0], x_ref[0]
    copies = []

    def start(source, target):
        copies.append(pltpu.make_async_copy(source, target, sems.at[len(copies)]))
        copies[-1].start()

    for i, (p, ahead) in enumerate(parts):
        x = (me + ahead) % NX
        start(blocks[i].at[:, pl.ds(0, ROWS)], kv_ref.at[p, x])
    for i, (p, ahead) in enumerate(parts):
        x = (me + ahead) % NX
        for z in range(NZ):
            for k in range(NT):
                if k:
                    at = ROWS + (k - 1) * SL
                    new = blocks[i][z, at : at + SL, :]
                else:
                    new = blocks[i][z, pl.ds(pl.multiple_of(tp * SL, SL), SL), :]
                lanes = pl.ds(pl.multiple_of(((tp + k) % NT) * COLS, COLS), COLS)
                old = avg_ref[p, x, z, :, lanes].astype(f32)
                blend_ref[i, z, :, lanes] = (0.8 * old + 0.2 * new.astype(f32)).astype(bf16)
            lines_ref[i, z : z + 1, :] = blocks[i][z, ROWS + AVG : ROWS + AVG + 1, :]
        start(blend_ref.at[i], avg_out_ref.at[p, x])
        start(lines_ref.at[i], gain_ref.at[p, x])
    for copy in copies:
        copy.wait()


def place(parts, blocks, tp, me, average, before):
    count = len(parts)
    smem, vmem, hbm = (
        pl.BlockSpec(memory_space=m) for m in (pltpu.SMEM, pltpu.VMEM, pltpu.HBM)
    )
    return pl.pallas_call(
        functools.partial(place_kernel, parts),
        in_specs=[smem, smem] + [vmem] * (1 + count) + [hbm] * len(before),
        out_specs=[hbm] * 3,
        out_shape=[
            jax.ShapeDtypeStruct((NY, NX, NZ, ROWS, COLS), bf16),
            jax.ShapeDtypeStruct((NY, NX, NZ, SL, NT * COLS), bf16),
            jax.ShapeDtypeStruct((NY, NX, NZ, COLS), bf16),
        ],
        input_output_aliases={3 + count + i: i for i in range(len(before))},
        scratch_shapes=[
            pltpu.VMEM((count, NZ, SL, NT * COLS), bf16),
            pltpu.VMEM((count, NZ, COLS), bf16),
            pltpu.SemaphoreType.DMA((3 * count,)),
        ],
        compiler_params=pltpu.CompilerParams(vmem_limit_bytes=8 << 20),
        cost_estimate=pl.CostEstimate(
            flops=count << 20, bytes_accessed=count << 19, transcendentals=0
        ),
    )(tp, me, average, *blocks, *before)


def spread(block, axes, count):
    return lax.all_to_all(
        jnp.broadcast_to(block[None], (count,) + block.shape), axes, 0, 0, tiled=True
    )


def call(kernel, outs, *args, smem=0):
    specs = [pl.BlockSpec(memory_space=pltpu.SMEM)] * smem
    specs += [pl.BlockSpec(memory_space=pltpu.VMEM)] * (len(args) - smem)
    moved = sum(a.size * a.dtype.itemsize for a in args)
    return pl.pallas_call(
        kernel,
        out_shape=[jax.ShapeDtypeStruct(s, d) for s, d in outs],
        in_specs=specs,
        out_specs=[pl.BlockSpec(memory_space=pltpu.VMEM)] * len(outs),
        compiler_params=pltpu.CompilerParams(vmem_limit_bytes=8 << 20),
        cost_estimate=pl.CostEstimate(flops=moved, bytes_accessed=moved, transcendentals=0),
    )(*args)


def shards(
    grad_kv,
    grad_gains,
    kv_weight,
    kv_first,
    kv_second,
    gain_weight,
    gain_first,
    gain_second,
    average,
):
    tp = lax.axis_index(T)
    slim = gain_weight.shape[0]
    at = tp.astype(jnp.int32).reshape(1)
    me = lax.axis_index("x").astype(jnp.int32).reshape(1)

    sent = jnp.concatenate(
        [
            grad_kv.reshape(NF, ROWS, COLS),
            grad_gains.reshape(NF, 1, COLS),
            jnp.zeros((NF, 7, COLS), bf16),
        ],
        axis=1,
    )
    sent, at, me = lax.optimization_barrier((sent, at, me))
    got = lax.all_to_all(sent, F, 0, 0, tiled=True)
    part, msg = call(
        sum_kernel,
        [((ROWS, COLS), f32), ((NT, MSG, COLS), f32)],
        at, got,
        gain_weight.reshape(1, slim), gain_first.reshape(1, slim), gain_second.reshape(1, slim),
        kv_weight, kv_first, kv_second,
        smem=1,
    )

    got = lax.all_to_all(msg, T, 0, 0, tiled=True)
    gain_rows, msg = call(norm_kernel, [((8, COLS), f32), ((NF, COLS), f32)], got)
    sums = lax.all_to_all(msg, F, 0, 0, tiled=True)

    kv_w, kv_m, kv_v, gain_w, gain_m, gain_v, block = call(
        update_kernel,
        [((ROWS, COLS), f32)] * 3 + [((1, slim), f32)] * 3 + [((BLOCK, COLS), bf16)],
        at, sums, part, kv_weight, kv_first, kv_second, got, gain_rows,
        smem=1,
    )

    block = spread(block, ("yh", "z"), NY * NZ).reshape(NY, NZ, BLOCK, COLS)
    ahead = [(i, (i + 1) % NX) for i in range(NX)]
    back = [(i, (i - 1) % NX) for i in range(NX)]
    half0, half1 = block[0], block[1]
    l0 = lax.ppermute(half0, "x", ahead)
    r1 = lax.ppermute(half1, "x", back)
    l1 = lax.ppermute(half1, "x", ahead)
    r0 = lax.ppermute(half0, "x", back)
    d0 = lax.ppermute(l0, "x", ahead)
    d1 = lax.ppermute(r1, "x", back)

    average_in = average.reshape(NY, NX, NZ, SL, NT * COLS)
    outs = place([(0, 0), (1, 0)], [half0, half1], at, me, average_in, ())
    outs = place(
        [(0, 3), (1, 1), (1, 3), (0, 1)], [l0, r1, l1, r0], at, me, average_in, outs
    )
    outs = place([(0, 2), (1, 2)], [d0, d1], at, me, average_in, outs)
    kv_blocks, average_out, gain_copy = outs
    return (
        kv_w, kv_m, kv_v, gain_w.reshape(-1), gain_m.reshape(-1), gain_v.reshape(-1),
        kv_blocks.reshape(-1, COLS), gain_copy.reshape(-1), average_out.reshape(average.shape),
    )


def solution(mesh):
    fine = Mesh(mesh.devices.reshape(NY, NX, NZ, 4, 2), F + T)
    in_specs = (
        P(F, None, T),
        P(F, T, None),
        P(F, T),
        P(F, T),
        P(F, T),
        P(F + T),
        P(F + T),
        P(F + T),
        P(None, T, None),
    )
    out_specs = (
        P(F, T),
        P(F, T),
        P(F, T),
        P(F + T),
        P(F + T),
        P(F + T),
        P(None, T),
        P(),
        P(None, T, None),
    )
    return jax.shard_map(shards, mesh=fine, in_specs=in_specs, out_specs=out_specs, check_vma=False)
```

```python
import functools

import jax
import jax.numpy as jnp
from jax import lax
from jax.experimental import pallas as pl
from jax.experimental.pallas import tpu as pltpu
from jax.sharding import Mesh, PartitionSpec as P

STEP = 100
PARAMS = 4202496
F = ("yh", "x", "z")
T = ("yl", "c")
NY, NX, NZ, NT = 2, 4, 8, 8
NF = NY * NX * NZ
ROWS, COLS = 64, 128
SL = ROWS // NT
PACK = ROWS + 8
STATE = SL + 8
MSG = STATE + 3 * SL
AVG = (NT - 1) * SL
BLOCK = ROWS + AVG + 8
f32, bf16 = jnp.float32, jnp.bfloat16


def adam_update(grad, first, second, weight, factor, decay):
    clipped = factor * grad
    first_new = 0.9 * first + 0.1 * clipped
    second_new = 0.95 * second + 0.05 * clipped * clipped
    first_fix = 1.0 - 0.9**STEP
    second_fix = 1.0 - 0.95**STEP
    step_dir = first_new / first_fix / (jnp.sqrt(second_new / second_fix) + 1e-08)
    weight_new = weight - 0.001 * (step_dir + decay * weight)
    return (weight_new, first_new, second_new)


def sum_kernel(
    tp_ref, got_ref, gw_ref, gm_ref, gv_ref, w_ref, m_ref, v_ref, part_ref, msg_ref
):
    square = jnp.zeros((SL, COLS), f32)
    for r in range(0, PACK, SL):
        acc = got_ref[0, r : r + SL, :].astype(f32)
        for s in range(1, NF):
            acc += got_ref[s, r : r + SL, :].astype(f32)
        if r < ROWS:
            part_ref[r : r + SL, :] = acc
            msg_ref[r // SL, :SL, :] = acc
            square += acc * acc
    at = lax.broadcasted_iota(jnp.int32, (8, COLS), 0)
    line = jnp.broadcast_to(jnp.sum(square, axis=0, keepdims=True), (8, COLS))
    slim = COLS // NT
    gains = jnp.concatenate([ref[...] for ref in (gw_ref, gm_ref, gv_ref)], axis=0)
    gains = jnp.concatenate([gains, jnp.zeros((3, COLS - slim), f32)], axis=1)
    gains = jnp.concatenate([jnp.zeros((2, COLS), f32), gains, jnp.zeros((3, COLS), f32)])
    gains = pltpu.roll(gains, tp_ref[0] * slim, 1)
    misc = jnp.where(at == 0, acc, jnp.where(at == 1, line, gains))
    for t in range(NT):
        msg_ref[t, SL:STATE, :] = misc
        for k, ref in enumerate((w_ref, m_ref, v_ref)):
            msg_ref[t, STATE + k * SL : STATE + (k + 1) * SL, :] = ref[t * SL : (t + 1) * SL, :]


def norm_kernel(got_ref, gain_ref, msg_ref):
    acc = got_ref[0, SL:STATE, :]
    for t in range(1, NT):
        acc += got_ref[t, SL:STATE, :]
    gain_ref[...] = acc
    line = acc[1:2] + acc[0:1] * acc[0:1]
    msg_ref[...] = jnp.broadcast_to(line, msg_ref.shape)


def update_kernel(
    tp_ref, sums_ref, part_ref, w0_ref, m0_ref, v0_ref, got_ref, gain_ref,
    w_ref, m_ref, v_ref, gw_ref, gm_ref, gv_ref, out_ref,
):
    total = jnp.sum(sums_ref[...])
    factor = jnp.minimum(
        f32(1.0), 1.0 / jnp.sqrt(jnp.full((1, COLS), total) / PARAMS + 1e-06)
    )
    tp = tp_ref[0]
    w, m, v = adam_update(
        part_ref[...], m0_ref[...], v0_ref[...], w0_ref[...], factor, 0.1
    )
    w_ref[...] = w
    m_ref[...] = m
    v_ref[...] = v
    out_ref[:ROWS, :] = w.astype(bf16)
    for k in range(1, NT):
        t = (tp + k) % NT
        old = [got_ref[t, STATE + j * SL : STATE + (j + 1) * SL, :] for j in range(3)]
        w, _, _ = adam_update(got_ref[t, :SL, :], old[1], old[2], old[0], factor, 0.1)
        at = ROWS + (k - 1) * SL
        out_ref[at : at + SL, :] = w.astype(bf16)
    rows = gain_ref[...]
    new = adam_update(rows[0:1], rows[3:4], rows[4:5], rows[2:3], factor, 0.0)
    slim = COLS // NT
    own = jnp.concatenate(list(new) + [jnp.zeros((5, COLS), f32)], axis=0)
    own = pltpu.roll(own, (COLS - tp * slim) % COLS, 1)
    for k, ref in enumerate((gw_ref, gm_ref, gv_ref)):
        ref[...] = own[k : k + 1, :slim]
    out_ref[ROWS + AVG :, :] = jnp.concatenate(
        [new[0], jnp.zeros((7, COLS), f32)], axis=0
    ).astype(bf16)


def place_kernel(parts, tp_ref, x_ref, avg_ref, *refs):
    count = len(parts)
    blocks = refs[:count]
    kv_ref, avg_out_ref, gain_ref, blend_ref, lines_ref, sems = refs[-6:]
    tp, me = tp_ref[0], x_ref[0]
    copies = []

    def start(source, target):
        copies.append(pltpu.make_async_copy(source, target, sems.at[len(copies)]))
        copies[-1].start()

    for i, (p, ahead) in enumerate(parts):
        x = (me + ahead) % NX
        start(blocks[i].at[:, pl.ds(0, ROWS)], kv_ref.at[p, x])
    for i, (p, ahead) in enumerate(parts):
        x = (me + ahead) % NX
        for z in range(NZ):
            for k in range(NT):
                if k:
                    at = ROWS + (k - 1) * SL
                    new = blocks[i][z, at : at + SL, :]
                else:
                    new = blocks[i][z, pl.ds(pl.multiple_of(tp * SL, SL), SL), :]
                lanes = pl.ds(pl.multiple_of(((tp + k) % NT) * COLS, COLS), COLS)
                old = avg_ref[p, x, z, :, lanes].astype(f32)
                blend_ref[i, z, :, lanes] = (0.8 * old + 0.2 * new.astype(f32)).astype(bf16)
            lines_ref[i, z : z + 1, :] = blocks[i][z, ROWS + AVG : ROWS + AVG + 1, :]
        start(blend_ref.at[i], avg_out_ref.at[p, x])
        start(lines_ref.at[i], gain_ref.at[p, x])
    for copy in copies:
        copy.wait()


def place(parts, blocks, tp, me, average, before):
    count = len(parts)
    smem, vmem, hbm = (
        pl.BlockSpec(memory_space=m) for m in (pltpu.SMEM, pltpu.VMEM, pltpu.HBM)
    )
    return pl.pallas_call(
        functools.partial(place_kernel, parts),
        in_specs=[smem, smem] + [vmem] * (1 + count) + [hbm] * len(before),
        out_specs=[hbm] * 3,
        out_shape=[
            jax.ShapeDtypeStruct((NY, NX, NZ, ROWS, COLS), bf16),
            jax.ShapeDtypeStruct((NY, NX, NZ, SL, NT * COLS), bf16),
            jax.ShapeDtypeStruct((NY, NX, NZ, COLS), bf16),
        ],
        input_output_aliases={3 + count + i: i for i in range(len(before))},
        scratch_shapes=[
            pltpu.VMEM((count, NZ, SL, NT * COLS), bf16),
            pltpu.VMEM((count, NZ, COLS), bf16),
            pltpu.SemaphoreType.DMA((3 * count,)),
        ],
        compiler_params=pltpu.CompilerParams(vmem_limit_bytes=8 << 20),
        cost_estimate=pl.CostEstimate(
            flops=count << 20, bytes_accessed=count << 19, transcendentals=0
        ),
    )(tp, me, average, *blocks, *before)


def spread(block, axes, count):
    return lax.all_to_all(
        jnp.broadcast_to(block[None], (count,) + block.shape), axes, 0, 0, tiled=True
    )


def call(kernel, outs, *args, smem=0):
    specs = [pl.BlockSpec(memory_space=pltpu.SMEM)] * smem
    specs += [pl.BlockSpec(memory_space=pltpu.VMEM)] * (len(args) - smem)
    moved = sum(a.size * a.dtype.itemsize for a in args)
    return pl.pallas_call(
        kernel,
        out_shape=[jax.ShapeDtypeStruct(s, d) for s, d in outs],
        in_specs=specs,
        out_specs=[pl.BlockSpec(memory_space=pltpu.VMEM)] * len(outs),
        compiler_params=pltpu.CompilerParams(vmem_limit_bytes=8 << 20),
        cost_estimate=pl.CostEstimate(flops=moved, bytes_accessed=moved, transcendentals=0),
    )(*args)


def shards(
    grad_kv,
    grad_gains,
    kv_weight,
    kv_first,
    kv_second,
    gain_weight,
    gain_first,
    gain_second,
    average,
):
    tp = lax.axis_index(T)
    slim = gain_weight.shape[0]
    at = tp.astype(jnp.int32).reshape(1)
    me = lax.axis_index("x").astype(jnp.int32).reshape(1)

    sent = jnp.concatenate(
        [
            grad_kv.reshape(NF, ROWS, COLS),
            grad_gains.reshape(NF, 1, COLS),
            jnp.zeros((NF, 7, COLS), bf16),
        ],
        axis=1,
    )
    sent, at, me = lax.optimization_barrier((sent, at, me))
    got = lax.all_to_all(sent, F, 0, 0, tiled=True)
    part, msg = call(
        sum_kernel,
        [((ROWS, COLS), f32), ((NT, MSG, COLS), f32)],
        at, got,
        gain_weight.reshape(1, slim), gain_first.reshape(1, slim), gain_second.reshape(1, slim),
        kv_weight, kv_first, kv_second,
        smem=1,
    )

    got = lax.all_to_all(msg, T, 0, 0, tiled=True)
    gain_rows, msg = call(norm_kernel, [((8, COLS), f32), ((NF, COLS), f32)], got)
    sums = lax.all_to_all(msg, F, 0, 0, tiled=True)

    kv_w, kv_m, kv_v, gain_w, gain_m, gain_v, block = call(
        update_kernel,
        [((ROWS, COLS), f32)] * 3 + [((1, slim), f32)] * 3 + [((BLOCK, COLS), bf16)],
        at, sums, part, kv_weight, kv_first, kv_second, got, gain_rows,
        smem=1,
    )

    block = spread(block, ("yh", "z"), NY * NZ).reshape(NY, NZ, BLOCK, COLS)
    ahead = [(i, (i + 1) % NX) for i in range(NX)]
    back = [(i, (i - 1) % NX) for i in range(NX)]
    half0, half1 = block[0], block[1]
    l0 = lax.ppermute(half0, "x", ahead)
    r1 = lax.ppermute(half1, "x", back)
    l1 = lax.ppermute(half1, "x", ahead)
    r0 = lax.ppermute(half0, "x", back)
    d0 = lax.ppermute(l0, "x", ahead)
    d1 = lax.ppermute(r1, "x", back)

    average_in = average.reshape(NY, NX, NZ, SL, NT * COLS)
    outs = place([(0, 0), (1, 0)], [half0, half1], at, me, average_in, ())
    outs = place(
        [(0, 3), (1, 1), (1, 3), (0, 1)], [l0, r1, l1, r0], at, me, average_in, outs
    )
    outs = place([(1, 2)], [d1], at, me, average_in, outs)
    outs = place([(0, 2)], [d0], at, me, average_in, outs)
    kv_blocks, average_out, gain_copy = outs
    return (
        kv_w, kv_m, kv_v, gain_w.reshape(-1), gain_m.reshape(-1), gain_v.reshape(-1),
        kv_blocks.reshape(-1, COLS), gain_copy.reshape(-1), average_out.reshape(average.shape),
    )


def solution(mesh):
    fine = Mesh(mesh.devices.reshape(NY, NX, NZ, 4, 2), F + T)
    in_specs = (
        P(F, None, T),
        P(F, T, None),
        P(F, T),
        P(F, T),
        P(F, T),
        P(F + T),
        P(F + T),
        P(F + T),
        P(None, T, None),
    )
    out_specs = (
        P(F, T),
        P(F, T),
        P(F, T),
        P(F + T),
        P(F + T),
        P(F + T),
        P(None, T),
        P(),
        P(None, T, None),
    )
    return jax.shard_map(shards, mesh=fine, in_specs=in_specs, out_specs=out_specs, check_vma=False)
```

```python
import functools

import jax
import jax.numpy as jnp
from jax import lax
from jax.experimental import pallas as pl
from jax.experimental.pallas import tpu as pltpu
from jax.sharding import Mesh, PartitionSpec as P

STEP = 100
PARAMS = 4202496
F = ("yh", "x", "z")
T = ("yl", "c")
NY, NX, NZ, NT = 2, 4, 8, 8
NF = NY * NX * NZ
ROWS, COLS = 64, 128
SL = ROWS // NT
PACK = ROWS + 8
STATE = SL + 8
MSG = STATE + 3 * SL
AVG = (NT - 1) * SL
BLOCK = ROWS + AVG + 8
f32, bf16 = jnp.float32, jnp.bfloat16


def adam_update(grad, first, second, weight, factor, decay):
    clipped = factor * grad
    first_new = 0.9 * first + 0.1 * clipped
    second_new = 0.95 * second + 0.05 * clipped * clipped
    first_fix = 1.0 - 0.9**STEP
    second_fix = 1.0 - 0.95**STEP
    step_dir = first_new / first_fix / (jnp.sqrt(second_new / second_fix) + 1e-08)
    weight_new = weight - 0.001 * (step_dir + decay * weight)
    return (weight_new, first_new, second_new)


def sum_kernel(
    tp_ref, got_ref, gw_ref, gm_ref, gv_ref, w_ref, m_ref, v_ref, part_ref, msg_ref
):
    square = jnp.zeros((SL, COLS), f32)
    for r in range(0, PACK, SL):
        acc = got_ref[0, r : r + SL, :].astype(f32)
        for s in range(1, NF):
            acc += got_ref[s, r : r + SL, :].astype(f32)
        if r < ROWS:
            part_ref[r : r + SL, :] = acc
            msg_ref[r // SL, :SL, :] = acc
            square += acc * acc
    at = lax.broadcasted_iota(jnp.int32, (8, COLS), 0)
    line = jnp.broadcast_to(jnp.sum(square, axis=0, keepdims=True), (8, COLS))
    slim = COLS // NT
    gains = jnp.concatenate([ref[...] for ref in (gw_ref, gm_ref, gv_ref)], axis=0)
    gains = jnp.concatenate([gains, jnp.zeros((3, COLS - slim), f32)], axis=1)
    gains = jnp.concatenate([jnp.zeros((2, COLS), f32), gains, jnp.zeros((3, COLS), f32)])
    gains = pltpu.roll(gains, tp_ref[0] * slim, 1)
    misc = jnp.where(at == 0, acc, jnp.where(at == 1, line, gains))
    for t in range(NT):
        msg_ref[t, SL:STATE, :] = misc
        for k, ref in enumerate((w_ref, m_ref, v_ref)):
            msg_ref[t, STATE + k * SL : STATE + (k + 1) * SL, :] = ref[t * SL : (t + 1) * SL, :]


def norm_kernel(got_ref, gain_ref, msg_ref):
    acc = got_ref[0, SL:STATE, :]
    for t in range(1, NT):
        acc += got_ref[t, SL:STATE, :]
    gain_ref[...] = acc
    line = acc[1:2] + acc[0:1] * acc[0:1]
    msg_ref[...] = jnp.broadcast_to(line, msg_ref.shape)


def update_kernel(
    tp_ref, sums_ref, part_ref, w0_ref, m0_ref, v0_ref, got_ref, gain_ref,
    w_ref, m_ref, v_ref, gw_ref, gm_ref, gv_ref, out_ref,
):
    total = jnp.sum(sums_ref[...])
    factor = jnp.minimum(
        f32(1.0), 1.0 / jnp.sqrt(jnp.full((1, COLS), total) / PARAMS + 1e-06)
    )
    tp = tp_ref[0]
    w, m, v = adam_update(
        part_ref[...], m0_ref[...], v0_ref[...], w0_ref[...], factor, 0.1
    )
    w_ref[...] = w
    m_ref[...] = m
    v_ref[...] = v
    out_ref[:ROWS, :] = w.astype(bf16)
    for k in range(1, NT):
        t = (tp + k) % NT
        old = [got_ref[t, STATE + j * SL : STATE + (j + 1) * SL, :] for j in range(3)]
        w, _, _ = adam_update(got_ref[t, :SL, :], old[1], old[2], old[0], factor, 0.1)
        at = ROWS + (k - 1) * SL
        out_ref[at : at + SL, :] = w.astype(bf16)
    rows = gain_ref[...]
    new = adam_update(rows[0:1], rows[3:4], rows[4:5], rows[2:3], factor, 0.0)
    slim = COLS // NT
    own = jnp.concatenate(list(new) + [jnp.zeros((5, COLS), f32)], axis=0)
    own = pltpu.roll(own, (COLS - tp * slim) % COLS, 1)
    for k, ref in enumerate((gw_ref, gm_ref, gv_ref)):
        ref[...] = own[k : k + 1, :slim]
    out_ref[ROWS + AVG :, :] = jnp.concatenate(
        [new[0], jnp.zeros((7, COLS), f32)], axis=0
    ).astype(bf16)


def place_kernel(parts, before, tp_ref, x_ref, avg_ref, *refs):
    count = len(parts)
    given = len(refs) - 6 - (3 if before else 0)
    blocks = refs[:given]
    if given < count:
        blocks = [ref.at[p] for ref in blocks for p in range(NY)]
    kv_ref, avg_out_ref, gain_ref, blend_ref, lines_ref, sems = refs[-6:]
    tp, me = tp_ref[0], x_ref[0]
    copies = []

    def start(source, target):
        copies.append(pltpu.make_async_copy(source, target, sems.at[len(copies)]))
        copies[-1].start()

    for i, (p, ahead) in enumerate(parts):
        x = (me + ahead) % NX
        start(blocks[i].at[:, pl.ds(0, ROWS)], kv_ref.at[p, x])
    for i, (p, ahead) in enumerate(parts):
        x = (me + ahead) % NX
        for z in range(NZ):
            for k in range(NT):
                if k:
                    at = ROWS + (k - 1) * SL
                    new = blocks[i][z, at : at + SL, :]
                else:
                    new = blocks[i][z, pl.ds(pl.multiple_of(tp * SL, SL), SL), :]
                lanes = pl.ds(pl.multiple_of(((tp + k) % NT) * COLS, COLS), COLS)
                old = avg_ref[p, x, z, :, lanes].astype(f32)
                blend_ref[i, z, :, lanes] = (0.8 * old + 0.2 * new.astype(f32)).astype(bf16)
            lines_ref[i, z : z + 1, :] = blocks[i][z, ROWS + AVG : ROWS + AVG + 1, :]
        start(blend_ref.at[i], avg_out_ref.at[p, x])
        start(lines_ref.at[i], gain_ref.at[p, x])
    for copy in copies:
        copy.wait()


def place(parts, blocks, tp, me, average, before):
    count = len(parts)
    smem, vmem, hbm = (
        pl.BlockSpec(memory_space=m) for m in (pltpu.SMEM, pltpu.VMEM, pltpu.HBM)
    )
    return pl.pallas_call(
        functools.partial(place_kernel, parts, bool(before)),
        in_specs=[smem, smem] + [vmem] * (1 + len(blocks)) + [hbm] * len(before),
        out_specs=[hbm] * 3,
        out_shape=[
            jax.ShapeDtypeStruct((NY, NX, NZ, ROWS, COLS), bf16),
            jax.ShapeDtypeStruct((NY, NX, NZ, SL, NT * COLS), bf16),
            jax.ShapeDtypeStruct((NY, NX, NZ, COLS), bf16),
        ],
        input_output_aliases={3 + len(blocks) + i: i for i in range(len(before))},
        scratch_shapes=[
            pltpu.VMEM((count, NZ, SL, NT * COLS), bf16),
            pltpu.VMEM((count, NZ, COLS), bf16),
            pltpu.SemaphoreType.DMA((3 * count,)),
        ],
        compiler_params=pltpu.CompilerParams(vmem_limit_bytes=8 << 20),
        cost_estimate=pl.CostEstimate(
            flops=count << 20, bytes_accessed=count << 19, transcendentals=0
        ),
    )(tp, me, average, *blocks, *before)


def spread(block, axes, count):
    return lax.all_to_all(
        jnp.broadcast_to(block[None], (count,) + block.shape), axes, 0, 0, tiled=True
    )


def call(kernel, outs, *args, smem=0):
    specs = [pl.BlockSpec(memory_space=pltpu.SMEM)] * smem
    specs += [pl.BlockSpec(memory_space=pltpu.VMEM)] * (len(args) - smem)
    moved = sum(a.size * a.dtype.itemsize for a in args)
    return pl.pallas_call(
        kernel,
        out_shape=[jax.ShapeDtypeStruct(s, d) for s, d in outs],
        in_specs=specs,
        out_specs=[pl.BlockSpec(memory_space=pltpu.VMEM)] * len(outs),
        compiler_params=pltpu.CompilerParams(vmem_limit_bytes=8 << 20),
        cost_estimate=pl.CostEstimate(flops=moved, bytes_accessed=moved, transcendentals=0),
    )(*args)


def shards(
    grad_kv,
    grad_gains,
    kv_weight,
    kv_first,
    kv_second,
    gain_weight,
    gain_first,
    gain_second,
    average,
):
    tp = lax.axis_index(T)
    slim = gain_weight.shape[0]
    at = tp.astype(jnp.int32).reshape(1)
    me = lax.axis_index("x").astype(jnp.int32).reshape(1)

    sent = jnp.concatenate(
        [
            grad_kv.reshape(NF, ROWS, COLS),
            grad_gains.reshape(NF, 1, COLS),
            jnp.zeros((NF, 7, COLS), bf16),
        ],
        axis=1,
    )
    sent, at, me = lax.optimization_barrier((sent, at, me))
    got = lax.all_to_all(sent, F, 0, 0, tiled=True)
    part, msg = call(
        sum_kernel,
        [((ROWS, COLS), f32), ((NT, MSG, COLS), f32)],
        at, got,
        gain_weight.reshape(1, slim), gain_first.reshape(1, slim), gain_second.reshape(1, slim),
        kv_weight, kv_first, kv_second,
        smem=1,
    )

    got = lax.all_to_all(msg, T, 0, 0, tiled=True)
    gain_rows, msg = call(norm_kernel, [((8, COLS), f32), ((NF, COLS), f32)], got)
    sums = lax.all_to_all(msg, F, 0, 0, tiled=True)

    kv_w, kv_m, kv_v, gain_w, gain_m, gain_v, block = call(
        update_kernel,
        [((ROWS, COLS), f32)] * 3 + [((1, slim), f32)] * 3 + [((BLOCK, COLS), bf16)],
        at, sums, part, kv_weight, kv_first, kv_second, got, gain_rows,
        smem=1,
    )

    block = spread(block, ("yh", "z"), NY * NZ).reshape(NY, NZ, BLOCK, COLS)
    ahead = [(i, (i + 1) % NX) for i in range(NX)]
    back = [(i, (i - 1) % NX) for i in range(NX)]
    left = lax.ppermute(block, "x", ahead)
    right = lax.ppermute(block, "x", back)
    d0 = lax.ppermute(left[0], "x", ahead)
    d1 = lax.ppermute(right[1], "x", back)

    average_in = average.reshape(NY, NX, NZ, SL, NT * COLS)
    outs = place([(0, 0), (1, 0)], [block], at, me, average_in, ())
    outs = place([(0, 3), (1, 3), (0, 1), (1, 1)], [left, right], at, me, average_in, outs)
    outs = place([(0, 2), (1, 2)], [d0, d1], at, me, average_in, outs)
    kv_blocks, average_out, gain_copy = outs
    return (
        kv_w, kv_m, kv_v, gain_w.reshape(-1), gain_m.reshape(-1), gain_v.reshape(-1),
        kv_blocks.reshape(-1, COLS), gain_copy.reshape(-1), average_out.reshape(average.shape),
    )


def solution(mesh):
    fine = Mesh(mesh.devices.reshape(NY, NX, NZ, 4, 2), F + T)
    in_specs = (
        P(F, None, T),
        P(F, T, None),
        P(F, T),
        P(F, T),
        P(F, T),
        P(F + T),
        P(F + T),
        P(F + T),
        P(None, T, None),
    )
    out_specs = (
        P(F, T),
        P(F, T),
        P(F, T),
        P(F + T),
        P(F + T),
        P(F + T),
        P(None, T),
        P(),
        P(None, T, None),
    )
    return jax.shard_map(shards, mesh=fine, in_specs=in_specs, out_specs=out_specs, check_vma=False)
```
